256 devices in a mesh: blk: 32 (over x, z), uly: 8 (over y, core).
Axes of the slice: x: 4, y: 4, z: 8, core: 2. Of those that a mesh axis runs over, the one named last changes fastest.
Arguments:
- tokens: bfloat16 [12288, 3072], P(('blk', 'uly')), may hold values from -6 to 6
- mod_shift: float32 [3072], replicated, may hold values from -3 to 3
- mod_scale: float32 [3072], replicated, may hold values from -2 to 6
- out_gate: float32 [3072], replicated, may hold values from 0.5 to 1.5
- w_qkv: bfloat16 [3072, 24, 384], P(None, 'uly'), may hold values from -0.109375 to 0.109375
- w_out: bfloat16 [3072, 3072], P('uly'), may hold values from -0.109375 to 0.109375
- tile_map: int32 [32], replicated, may hold values from 0 to 31, as said below
- window_corner: int32 [32, 2], replicated, may hold values from 0 to 5, as said below
Outputs:
- mixed: bfloat16 [12288, 3072], P(('blk', 'uly'))
The draws below stay inside these ranges and needn't reach their ends.
Inputs may be any that keep to these rules, and one draw needn't show every extreme that they name: `tile_map`: A permutation of the tile positions; position j holds a grid tile whose number differs from j by at most 1. `window_corner`: each query tile's 3 x 3 window lies inside the grid and contains the grid tile that its own position holds.
All inputs are finite; a program needn't handle non-finite values.
Results may differ from the reference program's by a relative error of at most 0.02.
The reference program's roundings to bfloat16 on the way (of `normed`, `qkv`, `weights` and `attn`) count: a program that leaves them out, or rounds other values in their place, can miss the bound.
Values may be sent and summed in bfloat16 or wider, within the bound.
A program may use at most 128 MiB of HBM per device.

```python
import jax
import jax.numpy as jnp
from jax import lax

D = 3072
HEADS = 24
HD = 128
TILE = 384
WIN = 3
GW = 4
TILES = 32
GH = 8
TOKENS = 12288


def tile_layout(key):
    base_key = jax.random.fold_in(key, 4711)
    swap_key = jax.random.fold_in(base_key, 1)
    row_key = jax.random.fold_in(base_key, 2)
    col_key = jax.random.fold_in(base_key, 3)
    swaps = jax.random.randint(swap_key, (TILES // 2,), 0, 2)
    swaps = swaps.at[0].set(1)
    pairs = jnp.arange(TILES, dtype=jnp.int32).reshape(TILES // 2, 2)
    placed = jnp.where(swaps[:, None] == 1, pairs[:, ::-1], pairs).reshape(TILES)
    grid_row = placed // GW
    grid_col = placed % GW
    back_row = jax.random.randint(row_key, (TILES,), 0, WIN)
    back_col = jax.random.randint(col_key, (TILES,), 0, WIN)
    corner_row = jnp.clip(grid_row - back_row, 0, GH - WIN)
    corner_col = jnp.clip(grid_col - back_col, 0, GW - WIN)
    corners = jnp.stack([corner_row, corner_col], axis=1).astype(jnp.int32)
    return (placed.astype(jnp.int32), corners)


def draw_tile_map(key, part):
    return tile_layout(key)[0]


def draw_window_corner(key, part):
    return tile_layout(key)[1]


def draw_mod_scale(key, part):
    values = jnp.clip(0.5 * jax.random.normal(key, (D,), jnp.float32), -2.0, 2.0)
    return values.astype(jnp.float32)


def steps_of(key, dims, pieces, least, largest):
    def one(dim, parts):
        heights = jax.random.uniform(jax.random.fold_in(jax.random.fold_in(key, 6), dim), (parts,), jnp.float32, least / len(pieces), largest / len(pieces))
        return jnp.repeat(jnp.exp(heights), dims[dim] // parts).reshape((-1,) + (1,) * (len(dims) - dim - 1))

    gain = one(*pieces[0])
    for cut in pieces[1:]:
        gain = gain * one(*cut)
    return gain


def gaussian(stream_key, shape, scale, most, shards=(), held_as=jnp.bfloat16):
    drawn = jax.random.normal(stream_key, shape, jnp.float32) * scale
    if len(shards) > 0:
        drawn = steps_of(stream_key, shape, shards, -0.22, 0.18) * drawn
    return jnp.clip(drawn, min=-most, max=most).astype(held_as)


def setup_inputs(seed: int = 0) -> dict:
    seeds = jax.random.split(jax.random.key(seed), 9)
    tokens = gaussian(seeds[0], (TOKENS, D), 1.0, 6.0, ((0, 256),))
    mod_shift = gaussian(seeds[1], (D,), 0.5, 3.0, (), jnp.float32)
    mod_scale = draw_mod_scale(jax.random.fold_in(seeds[8], 71), 0)
    out_gate = jnp.clip(jax.random.uniform(seeds[3], (D,), jnp.float32, 0.5, 1.5), 0.5, 1.5)
    w_qkv = gaussian(seeds[4], (D, HEADS, 3 * HD), D ** -0.5, 0.109375, ((1, 8),))
    w_out = gaussian(seeds[5], (HEADS * HD, D), (HEADS * HD) ** -0.5, 0.109375, ((0, 8),))
    tile_map = draw_tile_map(jax.random.fold_in(seeds[8], 71), 0)
    window_corner = draw_window_corner(jax.random.fold_in(seeds[8], 71), 0)
    return dict(tokens=tokens, mod_shift=mod_shift, mod_scale=mod_scale, out_gate=out_gate, w_qkv=w_qkv, w_out=w_out, tile_map=tile_map, window_corner=window_corner)


def reference(tokens, mod_shift, mod_scale, out_gate, w_qkv, w_out, tile_map, window_corner):
    values_in = tokens.astype(jnp.float32)
    mean_row = lax.optimization_barrier(jnp.mean(values_in, axis=-1, keepdims=True))
    centred = values_in - mean_row
    variance = lax.optimization_barrier(jnp.mean(centred * centred, axis=-1, keepdims=True))
    normed = (centred * lax.rsqrt(variance + 1e-06) * (1.0 + mod_scale) + mod_shift).astype(jnp.bfloat16)
    qkv = jnp.dot(normed, w_qkv.reshape(D, HEADS * 3 * HD), preferred_element_type=jnp.float32).astype(jnp.bfloat16)
    qkv = qkv.reshape(TILES, TILE, HEADS, 3 * HD)
    positions = jnp.argsort(tile_map).astype(jnp.int32)
    offsets = jnp.arange(WIN, dtype=jnp.int32)

    def one_tile(index):
        corner = window_corner[index]
        grid_ids = ((corner[0] + offsets)[:, None] * GW + (corner[1] + offsets)[None, :]).reshape(-1)
        key_pos = positions[grid_ids]
        keyset = qkv[key_pos].reshape(WIN * WIN * TILE, HEADS, 3 * HD)
        queries = qkv[index][:, :, :HD].astype(jnp.float32)
        keys = keyset[:, :, HD:2 * HD].astype(jnp.float32)
        values = keyset[:, :, 2 * HD:].astype(jnp.float32)
        scores = jnp.einsum('qhd,khd->hqk', queries, keys) / jnp.sqrt(jnp.float32(HD))
        highest = lax.optimization_barrier(jnp.max(scores, axis=-1, keepdims=True))
        probs = jnp.exp(scores - highest)
        weights = lax.optimization_barrier(probs.astype(jnp.bfloat16)).astype(jnp.float32)
        numer = jnp.einsum('hqk,khd->hqd', weights, values)
        denom = lax.optimization_barrier(jnp.sum(probs, axis=-1, keepdims=True))
        result = (numer / denom).astype(jnp.bfloat16)
        return jnp.transpose(result, (1, 0, 2)).reshape(TILE, HEADS * HD)
    attn = lax.map(one_tile, jnp.arange(TILES, dtype=jnp.int32)).reshape(TOKENS, HEADS * HD)
    output = jnp.dot(attn, w_out, preferred_element_type=jnp.float32)
    return (out_gate * output).astype(jnp.bfloat16)
```

```python
import jax
import jax.numpy as jnp
from jax import lax
from jax.experimental import pallas as pl
from jax.experimental.pallas import tpu as pltpu
from jax.sharding import PartitionSpec as P

TILE = 384
WIN = 3
GW = 4
NX = 4
NZ = 8
NY = 4
HD = 128
MESH = pl.DeviceIdType.MESH
VMEM_LIMIT = 62 * 1024 * 1024


def push(src, dst, send_sem, recv_sem, blk, uly):
    return pltpu.make_async_remote_copy(
        src_ref=src,
        dst_ref=dst,
        send_sem=send_sem,
        recv_sem=recv_sem,
        device_id={"blk": blk, "uly": uly},
        device_id_type=MESH,
    )


def where_am_i():
    blk = lax.axis_index("blk")
    uly = lax.axis_index("uly")
    return blk, uly


def greet(peers):
    barrier = pltpu.get_barrier_semaphore()
    for blk, uly in peers:
        pl.semaphore_signal(
            barrier, inc=1, device_id={"blk": blk, "uly": uly}, device_id_type=MESH
        )
    pl.semaphore_wait(barrier, len(peers))


def project_kernel(x_ref, shift_ref, scale_ref, w_hbm, qkv_ref, xbuf, wbuf, wsem, ssem, rsem):
    blk, uly = where_am_i()
    y, c = uly // 2, uly % 2
    rows = x_ref.shape[0]
    half = x_ref.shape[1] // 2
    heads = w_hbm.shape[0]
    for h in range(heads):
        pltpu.make_async_copy(w_hbm.at[h], wbuf.at[h], wsem.at[h]).start()

    up = ((y + 1) % NY) * 2 + c
    dn = ((y + 3) % NY) * 2 + c
    opp = ((y + 2) % NY) * 2 + c
    mate = y * 2 + (1 - c)
    greet([(blk, up), (blk, dn), (blk, mate)])

    values = x_ref[...].astype(jnp.float32)
    mean = jnp.mean(values, axis=-1, keepdims=True)
    centred = values - mean
    var = jnp.mean(centred * centred, axis=-1, keepdims=True)
    normed = centred * lax.rsqrt(var + 1e-06) * (1.0 + scale_ref[...]) + shift_ref[...]

    def piece(u, k):
        return xbuf.at[pl.ds(pl.multiple_of(u * rows, 16), rows), pl.ds(k * half, half)]

    xbuf[pl.ds(pl.multiple_of(uly * rows, 16), rows), :] = normed.astype(xbuf.dtype)

    sent = []

    def send(u, k, to):
        copy = push(piece(u, k), piece(u, k), ssem.at[len(sent)], rsem.at[u, k], blk, to)
        copy.start()
        sent.append(copy)

    def arrive(u, k):
        push(piece(u, k), piece(u, k), ssem.at[0], rsem.at[u, k], blk, mate).wait_recv()

    for first in (0, 1):
        send(uly, first, up)
        send(uly, 1 - first, dn)
        send(uly, first, mate)
    arrive(dn, 0)
    send(dn, 0, up)
    send(dn, 0, mate)
    arrive(up, 1)
    send(up, 1, dn)
    send(up, 1, mate)
    arrive(dn, 1)
    send(dn, 1, mate)
    arrive(up, 0)
    send(up, 0, mate)
    arrive(opp, 0)
    send(opp, 0, mate)
    arrive(opp, 1)
    send(opp, 1, mate)
    for k in (0, 1):
        for step in range(NY):
            arrive(((y + step) % NY) * 2 + (1 - c), k)

    for h in range(heads):
        pltpu.make_async_copy(w_hbm.at[h], wbuf.at[h], wsem.at[h]).wait()
        result = jnp.dot(xbuf[...], wbuf[h], preferred_element_type=jnp.float32)
        for part in range(3):
            qkv_ref[h, part] = result[:, part * HD : (part + 1) * HD].astype(qkv_ref.dtype)
    for copy in sent:
        copy.wait_send()


def attend_kernel(
    map_ref, corner_ref, qkv_hbm, attn_ref,
    kv, qb, ob, back, scores, asem, qsem, kvsem, bsem, hsem, osem,
):
    blk, uly = where_am_i()
    y, c = uly // 2, uly % 2
    x, z = blk // NZ, blk % NZ
    line = x * NZ
    mate = y * 2 + (1 - c)

    peers = [(blk, mate), (((x + 1) % NX) * NZ + z, uly), (((x + 3) % NX) * NZ + z, uly)]
    for step in range(1, NZ):
        for core in (0, 1):
            peers.append((line + (z + step) % NZ, y * 2 + core))
    greet(peers)

    def give(src, dst, send_sem, recv_sem, to_blk, to_uly, is_self):
        @pl.when(jnp.logical_not(is_self))
        def _():
            push(src, dst, send_sem, recv_sem, to_blk, to_uly).start()

        @pl.when(is_self)
        def _():
            pltpu.make_async_copy(src, dst, recv_sem).start()

    def given(src, dst, send_sem, recv_sem, to_blk, to_uly, is_self):
        @pl.when(jnp.logical_not(is_self))
        def _():
            push(src, dst, send_sem, recv_sem, to_blk, to_uly).wait_send()

    def kv_out(h, part):
        zd = 4 * c + h
        core = z % 2
        return (
            qkv_hbm.at[h, 1 + part], kv.at[blk, part], asem.at[h, 1 + part], kvsem.at[blk, part],
            line + zd, y * 2 + core, jnp.logical_and(zd == z, core == c),
        )

    def q_out(h):
        zd = 4 * c + h
        core = z // 4
        return (
            qkv_hbm.at[h, 0], qb.at[z % 4], asem.at[h, 0], qsem.at[z % 4],
            line + zd, y * 2 + core, jnp.logical_and(zd == z, core == c),
        )

    for h in range(3):
        for part in (0, 1):
            give(*kv_out(h, part))
    for h in range(3):
        give(*q_out(h))

    owner = z % 4 != 3

    def kv_arrive(slot, part):
        push(
            kv.at[slot, part], kv.at[slot, part], hsem.at[0], kvsem.at[slot, part], blk, mate
        ).wait_recv()

    def kv_send(slot, part, index, to_blk, to_uly):
        push(
            kv.at[slot, part], kv.at[slot, part], hsem.at[index], kvsem.at[slot, part],
            to_blk, to_uly,
        ).start()

    def o_out(i):
        core = z // 4
        h = z % 4
        to_z = 4 * c + i
        return (
            ob.at[i], back.at[h], osem.at[i], bsem.at[h],
            line + to_z, y * 2 + core, jnp.logical_and(to_z == z, core == c),
        )

    @pl.when(owner)
    def _():
        x_up = ((x + 1) % NX) * NZ + z
        x_dn = ((x + 3) % NX) * NZ + z
        odd = (z + c) % 2
        mine = []
        for near, far in ((0, 1), (2, 7), (6, 3), (4, 5)):
            mine.append((z + near + odd * (far - near)) % NZ)
        count = 0
        for zs in mine:
            slot = line + zs
            kv_arrive(slot, 0)
            kv_send(slot, 0, count, x_up, uly)
            kv_arrive(slot, 1)
            kv_send(slot, 1, count + 1, x_dn, uly)
            kv_send(slot, 1, count + 2, x_up, uly)
            kv_send(slot, 0, count + 3, x_dn, uly)
            kv_send(slot, 0, count + 4, blk, mate)
            kv_send(slot, 1, count + 5, blk, mate)
            count += 6
        for zs in mine:
            below = ((x + 3) % NX) * NZ + zs
            above = ((x + 1) % NX) * NZ + zs
            kv_arrive(below, 0)
            kv_send(below, 0, count, x_up, uly)
            kv_send(below, 0, count + 1, blk, mate)
            kv_arrive(above, 1)
            kv_send(above, 1, count + 2, x_dn, uly)
            kv_send(above, 1, count + 3, blk, mate)
            kv_arrive(below, 1)
            kv_send(below, 1, count + 4, blk, mate)
            kv_arrive(above, 0)
            kv_send(above, 0, count + 5, blk, mate)
            count += 6
        for zs in mine:
            across = ((x + 2) % NX) * NZ + zs
            for part in (0, 1):
                kv_arrive(across, part)
                kv_send(across, part, count + part, blk, mate)
            count += 2
        for zs in mine:
            other = zs + 1 - 2 * (zs % 2)
            for step in range(NX):
                for part in (0, 1):
                    kv_arrive(((x + step) % NX) * NZ + other, part)
        for i in range(4):
            push(qb.at[i], qb.at[i], hsem.at[0], qsem.at[i], blk, mate).wait_recv()

        factor = 1.0 / (HD**0.5)

        def one_tile(i, _):
            position = line + 4 * c + i
            row0 = corner_ref[position * 2]
            col0 = corner_ref[position * 2 + 1]
            queries = qb[i]
            slots = []
            best = None
            for w in range(WIN * WIN):
                slot = map_ref[(row0 + w // WIN) * GW + col0 + w % WIN]
                slots.append(slot)
                s = lax.dot_general(
                    queries, kv[slot, 0], (((1,), (1,)), ((), ())),
                    preferred_element_type=jnp.float32,
                )
                scores[w] = s
                for n in range(TILE // HD):
                    part = s[:, n * HD : (n + 1) * HD]
                    best = part if best is None else jnp.maximum(best, part)
            highest = jnp.max(best, axis=-1, keepdims=True)
            total = jnp.zeros((TILE, HD), jnp.float32)
            accum = jnp.zeros((TILE, HD), jnp.float32)
            for w in range(WIN * WIN):
                probs = jnp.exp((scores[w] - highest) * factor)
                for n in range(TILE // HD):
                    total = total + probs[:, n * HD : (n + 1) * HD]
                accum = accum + jnp.dot(
                    probs.astype(jnp.bfloat16), kv[slots[w], 1],
                    preferred_element_type=jnp.float32,
                )
            denom = jnp.sum(total, axis=-1, keepdims=True)
            ob[i] = (accum / denom).astype(ob.dtype)
            give(*o_out(i))
            return 0

        lax.fori_loop(0, 4, one_tile, 0)

        for index in range(count):
            push(
                kv.at[0, 0], kv.at[0, 0], hsem.at[index], kvsem.at[0, 0], blk, mate
            ).wait_send()
        for i in range(4):
            given(*o_out(i))

    for h in range(3):
        push(back.at[h], back.at[h], hsem.at[0], bsem.at[h], blk, mate).wait_recv()
        attn_ref[h] = back[h]
    for h in range(3):
        for part in (0, 1):
            given(*kv_out(h, part))
        given(*q_out(h))


def output_kernel(
    attn_ref, w_ref, gate_ref, out_ref,
    lhs, acc, give_mate, from_mate, relay_out, relay_in, fin_out, fin_in,
    msem, mrsem, ssem, rsem,
):
    blk, uly = where_am_i()
    y, c = uly // 2, uly % 2
    rows = out_ref.shape[0]
    width = out_ref.shape[1]
    half = width // 2
    up = ((y + 1) % NY) * 2 + c
    dn = ((y + 3) % NY) * 2 + c
    mate = y * 2 + (1 - c)
    greet([(blk, up), (blk, dn), (blk, mate)])

    order = (2, 1, 3, 0)
    for which, core in ((0, 1 - c), (1, c)):
        for n, step in enumerate(order):
            u = ((y + step) % NY) * 2 + core
            for h in range(3):
                lhs[which, pl.ds(n * rows, rows), pl.ds(h * HD, HD)] = attn_ref[
                    h, pl.ds(pl.multiple_of(u * rows, 16), rows), :
                ]

    part = jnp.dot(lhs[0], w_ref[...], preferred_element_type=jnp.float32)
    give_mate[...] = part.astype(give_mate.dtype).reshape(give_mate.shape)
    mates = []
    for n in range(4):
        copy = push(give_mate.at[n], from_mate.at[n], msem.at[n], mrsem.at[n], blk, mate)
        copy.start()
        mates.append(copy)
    acc[...] = jnp.dot(lhs[1], w_ref[...], preferred_element_type=jnp.float32).reshape(acc.shape)

    def cols(k):
        return slice(k * half, (k + 1) * half)

    def mixed(n, k):
        return acc[n, :, cols(k)] + from_mate[n, :, cols(k)].astype(jnp.float32)

    mates[0].wait_recv()
    sent = []
    for k, to in ((0, up), (1, dn)):
        relay_out[k] = mixed(0, k).astype(relay_out.dtype)
        copy = push(relay_out.at[k], relay_in.at[k], ssem.at[k], rsem.at[k], blk, to)
        copy.start()
        sent.append(copy)
    mates[1].wait_recv()
    mates[2].wait_recv()
    for d, to in ((0, up), (1, dn)):
        k = 1 - d
        fin_out[d, k] = mixed(1 + d, k).astype(fin_out.dtype)
        copy = push(
            fin_out.at[d, k], fin_in.at[d, k], ssem.at[2 + d * 2 + k], rsem.at[2 + d * 2 + k], blk, to
        )
        copy.start()
        sent.append(copy)
    for d, to in ((0, up), (1, dn)):
        k = d
        sent[k].wait_recv()
        fin_out[d, k] = (mixed(1 + d, k) + relay_in[k].astype(jnp.float32)).astype(fin_out.dtype)
        copy = push(
            fin_out.at[d, k], fin_in.at[d, k], ssem.at[2 + d * 2 + k], rsem.at[2 + d * 2 + k], blk, to
        )
        copy.start()
        sent.append(copy)
    mates[3].wait_recv()
    for copy in sent[2:]:
        copy.wait_recv()
    for k in (0, 1):
        total = mixed(3, k) + fin_in[0, k].astype(jnp.float32) + fin_in[1, k].astype(jnp.float32)
        out_ref[:, cols(k)] = (gate_ref[:, cols(k)] * total).astype(out_ref.dtype)
    for copy in sent + mates:
        copy.wait_send()


def vmem():
    return pl.BlockSpec(memory_space=pltpu.VMEM)


def hbm():
    return pl.BlockSpec(memory_space=pl.ANY)


def smem():
    return pl.BlockSpec(memory_space=pltpu.SMEM)


def params(collective_id):
    return pltpu.CompilerParams(
        collective_id=collective_id, has_side_effects=True, vmem_limit_bytes=VMEM_LIMIT
    )


def on_device(tokens, mod_shift, mod_scale, out_gate, w_qkv, w_out, tile_map, window_corner):
    rows, width = tokens.shape
    heads = w_qkv.shape[1]
    bf16 = jnp.bfloat16
    dma = pltpu.SemaphoreType.DMA
    qkv = pl.pallas_call(
        project_kernel,
        out_shape=jax.ShapeDtypeStruct((heads, 3, TILE, HD), bf16),
        in_specs=[vmem(), vmem(), vmem(), hbm()],
        out_specs=vmem(),
        scratch_shapes=[
            pltpu.VMEM((TILE, width), bf16),
            pltpu.VMEM((heads, width, 3 * HD), bf16),
            dma((3,)),
            dma((14,)),
            dma((8, 2)),
        ],
        compiler_params=params(0),
        name="project",
    )(tokens, mod_shift[None, :], mod_scale[None, :], jnp.transpose(w_qkv, (1, 0, 2)))

    attn = pl.pallas_call(
        attend_kernel,
        out_shape=jax.ShapeDtypeStruct((heads, TILE, HD), bf16),
        in_specs=[smem(), smem(), hbm()],
        out_specs=vmem(),
        scratch_shapes=[
            pltpu.VMEM((NX * NZ, 2, TILE, HD), bf16),
            pltpu.VMEM((4, TILE, HD), bf16),
            pltpu.VMEM((4, TILE, HD), bf16),
            pltpu.VMEM((3, TILE, HD), bf16),
            pltpu.VMEM((WIN * WIN, TILE, TILE), jnp.float32),
            dma((3, 3)),
            dma((4,)),
            dma((NX * NZ, 2)),
            dma((3,)),
            dma((56,)),
            dma((4,)),
        ],
        compiler_params=params(1),
        name="attend",
    )(tile_map, window_corner.reshape(-1), qkv)

    return pl.pallas_call(
        output_kernel,
        out_shape=jax.ShapeDtypeStruct((rows, width), bf16),
        in_specs=[vmem(), vmem(), vmem()],
        out_specs=vmem(),
        scratch_shapes=[
            pltpu.VMEM((2, 4 * rows, heads * HD), bf16),
            pltpu.VMEM((4, rows, width), jnp.float32),
            pltpu.VMEM((4, rows, width), bf16),
            pltpu.VMEM((4, rows, width), bf16),
            pltpu.VMEM((2, rows, width // 2), bf16),
            pltpu.VMEM((2, rows, width // 2), bf16),
            pltpu.VMEM((2, 2, rows, width // 2), bf16),
            pltpu.VMEM((2, 2, rows, width // 2), bf16),
            dma((4,)),
            dma((4,)),
            dma((6,)),
            dma((6,)),
        ],
        compiler_params=params(2),
        name="output",
    )(attn, w_out, out_gate[None, :])


def solution(mesh):
    in_specs = (
        P(("blk", "uly"), None),
        P(),
        P(),
        P(),
        P(None, "uly", None),
        P("uly", None),
        P(),
        P(),
    )
    out_specs = P(("blk", "uly"), None)
    return jax.shard_map(
        on_device, mesh=mesh, in_specs=in_specs, out_specs=out_specs, check_vma=False
    )
```

```python
import jax
import jax.numpy as jnp
from jax import lax
from jax.experimental import pallas as pl
from jax.experimental.pallas import tpu as pltpu
from jax.sharding import PartitionSpec as P

TILE = 384
WIN = 3
GW = 4
NX = 4
NZ = 8
NY = 4
HD = 128
MESH = pl.DeviceIdType.MESH
VMEM_LIMIT = 62 * 1024 * 1024


def push(src, dst, send_sem, recv_sem, blk, uly):
    return pltpu.make_async_remote_copy(
        src_ref=src,
        dst_ref=dst,
        send_sem=send_sem,
        recv_sem=recv_sem,
        device_id={"blk": blk, "uly": uly},
        device_id_type=MESH,
    )


def block_kernel(
    map_ref, corner_ref, x_ref, shift_ref, scale_ref, gate_ref, w_hbm, wo_hbm, out_ref,
    xbuf, wkv, wq, wo, stage, kv, qb, ob, back, scores,
    lhs, acc, give_mate, from_mate, relay_out, relay_in, fin_out, fin_in,
    wsem, wosem, gsem, grsem, asem, aqsem, kvsem, acrsem, matesem, fsem, qsem, bsem, osem,
    msem, mrsem, ssem, rsem,
):
    blk = lax.axis_index("blk")
    uly = lax.axis_index("uly")
    y, c = uly // 2, uly % 2
    x, z = blk // NZ, blk % NZ
    line = x * NZ
    rows, width = x_ref.shape
    half = width // 2
    chunk = 2 * rows
    heads = w_hbm.shape[0]
    up = ((y + 1) % NY) * 2 + c
    dn = ((y + 3) % NY) * 2 + c
    opp = ((y + 2) % NY) * 2 + c
    mate = y * 2 + (1 - c)
    x_up = ((x + 1) % NX) * NZ + z
    x_dn = ((x + 3) % NX) * NZ + z
    owner = z % 4 != 3

    weights = []
    for h in range(heads):
        weights.append(
            pltpu.make_async_copy(w_hbm.at[h, :, pl.ds(HD, 2 * HD)], wkv.at[h], wsem.at[h])
        )
    for h in range(heads):
        weights.append(
            pltpu.make_async_copy(
                w_hbm.at[h, :, pl.ds(0, HD)], wq.at[:, pl.ds(h * HD, HD)], wsem.at[heads + h]
            )
        )
    weights.append(pltpu.make_async_copy(wo_hbm, wo, wosem))
    for copy in weights:
        copy.start()

    peers = [(blk, mate), (blk, up), (blk, dn), (x_up, uly), (x_dn, uly)]
    for step in range(1, NZ):
        for core in (0, 1):
            peers.append((line + (z + step) % NZ, y * 2 + core))
    barrier = pltpu.get_barrier_semaphore()
    for to_blk, to_uly in peers:
        pl.semaphore_signal(
            barrier, inc=1, device_id={"blk": to_blk, "uly": to_uly}, device_id_type=MESH
        )

    values = x_ref[...].astype(jnp.float32)
    mean = jnp.mean(values, axis=-1, keepdims=True)
    centred = values - mean
    var = jnp.mean(centred * centred, axis=-1, keepdims=True)
    normed = centred * lax.rsqrt(var + 1e-06) * (1.0 + scale_ref[...]) + shift_ref[...]
    xbuf[pl.ds(pl.multiple_of(uly * rows, 16), rows), :] = normed.astype(xbuf.dtype)

    pl.semaphore_wait(barrier, len(peers))

    def piece(u, k):
        return xbuf.at[pl.ds(pl.multiple_of(u * rows, 16), rows), pl.ds(k * half, half)]

    gathered = []

    def spread(u, k, to):
        copy = push(piece(u, k), piece(u, k), gsem.at[len(gathered)], grsem.at[u, k], blk, to)
        copy.start()
        gathered.append(copy)

    def arrive(u, k):
        push(piece(u, k), piece(u, k), gsem.at[0], grsem.at[u, k], blk, mate).wait_recv()

    def chunk_rows(step):
        return pl.ds(pl.multiple_of(((y + step) % NY) * chunk, 16), chunk)

    def give(src, dst, send_sem, recv_sem, to_blk, to_uly, is_self):
        @pl.when(jnp.logical_not(is_self))
        def _():
            push(src, dst, send_sem, recv_sem, to_blk, to_uly).start()

        @pl.when(is_self)
        def _():
            pltpu.make_async_copy(src, dst, recv_sem).start()

    def given(src, dst, send_sem, recv_sem, to_blk, to_uly, is_self):
        @pl.when(jnp.logical_not(is_self))
        def _():
            push(src, dst, send_sem, recv_sem, to_blk, to_uly).wait_send()

    def turn(n):
        return (z + n) % heads

    def kv_out(n, step):
        h = turn(n)
        zd = 4 * c + h
        core = z % 2
        at = chunk_rows(step)
        return (
            stage.at[h, pl.ds(1, 2), at], kv.at[blk, :, at], asem.at[n, step],
            kvsem.at[blk, (y + step) % NY],
            line + zd, y * 2 + core, jnp.logical_and(zd == z, core == c),
        )

    def q_out(n):
        h = turn(n)
        zd = 4 * c + h
        core = z // 4
        return (
            stage.at[h, 0], qb.at[z % 4], aqsem.at[n], qsem.at[z % 4],
            line + zd, y * 2 + core, jnp.logical_and(zd == z, core == c),
        )

    def project(steps):
        left = jnp.concatenate([xbuf[chunk_rows(step), :] for step in steps], axis=0)
        for h in range(heads):
            result = jnp.dot(left, wkv[h], preferred_element_type=jnp.float32)
            for n, step in enumerate(steps):
                for part in (0, 1):
                    stage[h, 1 + part, chunk_rows(step), :] = result[
                        n * chunk : (n + 1) * chunk, part * HD : (part + 1) * HD
                    ].astype(stage.dtype)
        for step in steps:
            for n in range(heads):
                give(*kv_out(n, step))

    odd = (z + c) % 2
    mine = []
    for even_gap, odd_gap in ((0, 1), (2, 7), (6, 3), (4, 5)):
        mine.append((z + even_gap + odd * (odd_gap - even_gap)) % NZ)
    X_UP, X_DN, MATE_LINE, MATE_BELOW, MATE_ABOVE, RELAY_UP, RELAY_DN, MATE_ACROSS = range(8)

    def kv_part(slot, step, part):
        at = chunk_rows(step)
        if part is None:
            return kv.at[slot, :, at]
        return kv.at[slot, part, at]

    def kv_wait(slot, step):
        ref = kv_part(slot, step, None)
        push(ref, ref, fsem.at[0], kvsem.at[slot, (y + step) % NY], blk, mate).wait_recv()

    def kv_pass(slot, step, kind, to_blk, to_uly, recv_sem, part=None):
        ref = kv_part(slot, step, part)
        push(ref, ref, fsem.at[kind], recv_sem, to_blk, to_uly).start()

    def pump_line(step):
        n = (y + step) % NY
        for zs in mine:
            slot = line + zs
            kv_wait(slot, step)
            kv_pass(slot, step, X_UP, x_up, uly, kvsem.at[slot, n])
            kv_pass(slot, step, X_DN, x_dn, uly, kvsem.at[slot, n])
            kv_pass(slot, step, MATE_LINE, blk, mate, matesem)

    def pump_sides(step):
        n = (y + step) % NY
        for zs in mine:
            below = ((x + 3) % NX) * NZ + zs
            above = ((x + 1) % NX) * NZ + zs
            kv_wait(below, step)
            kv_pass(below, step, RELAY_UP, x_up, uly, acrsem.at[zs, n, 0], part=0)
            kv_pass(below, step, MATE_BELOW, blk, mate, matesem)
            kv_wait(above, step)
            kv_pass(above, step, RELAY_DN, x_dn, uly, acrsem.at[zs, n, 1], part=1)
            kv_pass(above, step, MATE_ABOVE, blk, mate, matesem)

    def pump_across(step):
        n = (y + step) % NY
        for zs in mine:
            across = ((x + 2) % NX) * NZ + zs
            for part in (0, 1):
                ref = kv_part(across, step, part)
                push(ref, ref, fsem.at[0], acrsem.at[zs, n, part], blk, mate).wait_recv()
                kv_pass(across, step, MATE_ACROSS, blk, mate, matesem, part=part)

    for first in (0, 1):
        spread(uly, first, up)
        spread(uly, 1 - first, dn)
        spread(uly, first, mate)
    for k in (0, 1):
        arrive(mate, k)
    for h in range(heads):
        weights[h].wait()
    project((0,))

    def mate_of(u):
        return u + 1 - 2 * c

    arrive(dn, 0)
    spread(dn, 0, up)
    spread(dn, 0, mate)
    arrive(up, 1)
    spread(up, 1, dn)
    spread(up, 1, mate)
    arrive(dn, 1)
    spread(dn, 1, mate)
    arrive(up, 0)
    spread(up, 0, mate)
    for k in (0, 1):
        arrive(mate_of(dn), k)
        arrive(mate_of(up), k)
    project((3, 1))

    @pl.when(owner)
    def _():
        pump_line(0)

    arrive(opp, 0)
    spread(opp, 0, mate)
    arrive(opp, 1)
    spread(opp, 1, mate)
    for k in (0, 1):
        arrive(mate_of(opp), k)
    project((2,))
    for h in range(heads):
        weights[heads + h].wait()
    result = jnp.dot(xbuf[...], wq[...], preferred_element_type=jnp.float32)
    for h in range(heads):
        stage[h, 0] = result[:, h * HD : (h + 1) * HD].astype(stage.dtype)
    for n in range(heads):
        give(*q_out(n))

    def o_out(i):
        core = z // 4
        h = z % 4
        to_z = 4 * c + i
        return (
            ob.at[i], back.at[h], osem.at[i], bsem.at[h],
            line + to_z, y * 2 + core, jnp.logical_and(to_z == z, core == c),
        )

    @pl.when(owner)
    def _():
        pump_line(3)
        pump_line(1)
        pump_sides(0)
        pump_line(2)
        pump_sides(3)
        pump_sides(1)
        pump_across(0)
        pump_sides(2)
        pump_across(3)
        pump_across(1)
        pump_across(2)
        sixteen = kv.at[pl.ds(0, 16)]
        push(sixteen, sixteen, fsem.at[0], matesem, blk, mate).wait_recv()
        for i in range(4):
            push(qb.at[i], qb.at[i], fsem.at[0], qsem.at[i], blk, mate).wait_recv()

        factor = 1.0 / (HD**0.5)

        def one_tile(n, _):
            i = (n + z) % 4
            position = line + 4 * c + i
            row0 = corner_ref[0, position]
            col0 = corner_ref[1, position]
            queries = qb[i]
            slots = []
            best = None
            for w in range(WIN * WIN):
                slot = map_ref[(row0 + w // WIN) * GW + col0 + w % WIN]
                slots.append(slot)
                s = lax.dot_general(
                    queries, kv[slot, 0], (((1,), (1,)), ((), ())),
                    preferred_element_type=jnp.float32,
                )
                scores[w] = s
                for n3 in range(TILE // HD):
                    part = s[:, n3 * HD : (n3 + 1) * HD]
                    best = part if best is None else jnp.maximum(best, part)
            highest = jnp.max(best, axis=-1, keepdims=True)
            total = jnp.zeros((TILE, HD), jnp.float32)
            accum = jnp.zeros((TILE, HD), jnp.float32)
            for w in range(WIN * WIN):
                probs = jnp.exp((scores[w] - highest) * factor)
                for n3 in range(TILE // HD):
                    total = total + probs[:, n3 * HD : (n3 + 1) * HD]
                accum = accum + jnp.dot(
                    probs.astype(jnp.bfloat16), kv[slots[w], 1],
                    preferred_element_type=jnp.float32,
                )
            denom = jnp.sum(total, axis=-1, keepdims=True)
            ob[i] = (accum / denom).astype(ob.dtype)
            give(*o_out(i))
            return 0

        lax.fori_loop(0, 4, one_tile, 0)

    weights[-1].wait()
    for h in range(heads):
        push(back.at[h], back.at[h], fsem.at[0], bsem.at[h], blk, mate).wait_recv()
    order = (2, 1, 3, 0)
    for which, core in ((0, 1 - c), (1, c)):
        for n, step in enumerate(order):
            u = ((y + step) % NY) * 2 + core
            for h in range(heads):
                lhs[which, pl.ds(n * rows, rows), pl.ds(h * HD, HD)] = back[
                    h, pl.ds(pl.multiple_of(u * rows, 16), rows), :
                ]

    part = jnp.dot(lhs[0], wo[...], preferred_element_type=jnp.float32)
    give_mate[...] = part.astype(give_mate.dtype).reshape(give_mate.shape)
    mates = []
    for n in range(4):
        copy = push(give_mate.at[n], from_mate.at[n], msem.at[n], mrsem.at[n], blk, mate)
        copy.start()
        mates.append(copy)
    acc[...] = jnp.dot(lhs[1], wo[...], preferred_element_type=jnp.float32).reshape(acc.shape)

    def cols(k):
        return slice(k * half, (k + 1) * half)

    def mixed(n, k):
        return acc[n, :, cols(k)] + from_mate[n, :, cols(k)].astype(jnp.float32)

    mates[0].wait_recv()
    sent = []
    for k, to in ((0, up), (1, dn)):
        relay_out[k] = mixed(0, k).astype(relay_out.dtype)
        copy = push(relay_out.at[k], relay_in.at[k], ssem.at[k], rsem.at[k], blk, to)
        copy.start()
        sent.append(copy)
    mates[1].wait_recv()
    mates[2].wait_recv()

    def finish(d, k, to, extra):
        value = mixed(1 + d, k)
        if extra is not None:
            value = value + extra
        fin_out[d, k] = value.astype(fin_out.dtype)
        n = 2 + d * 2 + k
        copy = push(fin_out.at[d, k], fin_in.at[d, k], ssem.at[n], rsem.at[n], blk, to)
        copy.start()
        sent.append(copy)

    for d, to in ((0, up), (1, dn)):
        finish(d, 1 - d, to, None)
    for d, to in ((0, up), (1, dn)):
        sent[d].wait_recv()
        finish(d, d, to, relay_in[d].astype(jnp.float32))
    mates[3].wait_recv()
    for copy in sent[2:]:
        copy.wait_recv()
    for k in (0, 1):
        total = mixed(3, k) + fin_in[0, k].astype(jnp.float32) + fin_in[1, k].astype(jnp.float32)
        out_ref[:, cols(k)] = (gate_ref[:, cols(k)] * total).astype(out_ref.dtype)

    for copy in gathered + sent + mates:
        copy.wait_send()
    for n in range(heads):
        for step in range(NY):
            given(*kv_out(n, step))
        given(*q_out(n))

    @pl.when(owner)
    def _():
        for kind in range(8):
            tiles = 2 if kind in (RELAY_UP, RELAY_DN) else 4
            ref = kv.at[pl.ds(0, tiles)]
            push(ref, ref, fsem.at[kind], matesem, blk, mate).wait_send()
        for i in range(4):
            given(*o_out(i))


def vmem():
    return pl.BlockSpec(memory_space=pltpu.VMEM)


def hbm():
    return pl.BlockSpec(memory_space=pl.ANY)


def smem():
    return pl.BlockSpec(memory_space=pltpu.SMEM)


def on_device(tokens, mod_shift, mod_scale, out_gate, w_qkv, w_out, tile_map, window_corner):
    rows, width = tokens.shape
    heads = w_qkv.shape[1]
    bf16 = jnp.bfloat16
    f32 = jnp.float32
    dma = pltpu.SemaphoreType.DMA
    return pl.pallas_call(
        block_kernel,
        out_shape=jax.ShapeDtypeStruct((rows, width), bf16),
        in_specs=[smem(), smem(), vmem(), vmem(), vmem(), vmem(), hbm(), hbm()],
        out_specs=vmem(),
        scratch_shapes=[
            pltpu.VMEM((TILE, width), bf16),
            pltpu.VMEM((heads, width, 2 * HD), bf16),
            pltpu.VMEM((width, heads * HD), bf16),
            pltpu.VMEM((heads * HD, width), bf16),
            pltpu.VMEM((heads, 3, TILE, HD), bf16),
            pltpu.VMEM((NX * NZ, 2, TILE, HD), bf16),
            pltpu.VMEM((4, TILE, HD), bf16),
            pltpu.VMEM((4, TILE, HD), bf16),
            pltpu.VMEM((heads, TILE, HD), bf16),
            pltpu.VMEM((WIN * WIN, TILE, TILE), f32),
            pltpu.VMEM((2, 4 * rows, heads * HD), bf16),
            pltpu.VMEM((4, rows, width), f32),
            pltpu.VMEM((4, rows, width), bf16),
            pltpu.VMEM((4, rows, width), bf16),
            pltpu.VMEM((2, rows, width // 2), bf16),
            pltpu.VMEM((2, rows, width // 2), bf16),
            pltpu.VMEM((2, 2, rows, width // 2), bf16),
            pltpu.VMEM((2, 2, rows, width // 2), bf16),
            dma((6,)),
            dma,
            dma((14,)),
            dma((8, 2)),
            dma((3, 4)),
            dma((3,)),
            dma((NX * NZ, 4)),
            dma((NZ, 4, 2)),
            dma,
            dma((8,)),
            dma((4,)),
            dma((3,)),
            dma((4,)),
            dma((4,)),
            dma((4,)),
            dma((6,)),
            dma((6,)),
        ],
        compiler_params=pltpu.CompilerParams(
            collective_id=0, has_side_effects=True, vmem_limit_bytes=VMEM_LIMIT
        ),
        name="block",
    )(
        tile_map, window_corner.T, tokens, mod_shift[None, :], mod_scale[None, :],
        out_gate[None, :], jnp.transpose(w_qkv, (1, 0, 2)), w_out,
    )


def solution(mesh):
    in_specs = (
        P(("blk", "uly"), None),
        P(),
        P(),
        P(),
        P(None, "uly", None),
        P("uly", None),
        P(),
        P(),
    )
    out_specs = P(("blk", "uly"), None)
    return jax.shard_map(
        on_device, mesh=mesh, in_specs=in_specs, out_specs=out_specs, check_vma=False
    )
```

```python
import jax
import jax.numpy as jnp
from jax import lax
from jax.experimental import pallas as pl
from jax.experimental.pallas import tpu as pltpu
from jax.sharding import PartitionSpec as P

TILE = 384
WIN = 3
GW = 4
NX = 4
NZ = 8
NY = 4
HD = 128
MESH = pl.DeviceIdType.MESH
VMEM_LIMIT = 62 * 1024 * 1024


def push(src, dst, send_sem, recv_sem, blk, uly):
    return pltpu.make_async_remote_copy(
        src_ref=src,
        dst_ref=dst,
        send_sem=send_sem,
        recv_sem=recv_sem,
        device_id={"blk": blk, "uly": uly},
        device_id_type=MESH,
    )


def block_kernel(
    map_ref, corner_ref, x_ref, shift_ref, scale_ref, gate_ref, w_hbm, wo_hbm, out_ref,
    xbuf, wkv, wq, wo, stage, kv, qb, ob_first, ob_last, edge_out, back, scores,
    lhs, acc, give_mate, from_mate, relay_out, relay_in, fin_out, fin_in,
    wsem, wosem, gsem, grsem, asem, aqsem, kvsem, matesem, fsem, qsem, bsem, osem,
    qxsem, qxrsem, oxsem, oxrsem, msem, mrsem, ssem, rsem,
):
    blk = lax.axis_index("blk")
    uly = lax.axis_index("uly")
    y, c = uly // 2, uly % 2
    x, z = blk // NZ, blk % NZ
    line = x * NZ
    rows, width = x_ref.shape
    half = width // 2
    chunk = 2 * rows
    heads = w_hbm.shape[0]
    up = ((y + 1) % NY) * 2 + c
    dn = ((y + 3) % NY) * 2 + c
    opp = ((y + 2) % NY) * 2 + c
    mate = y * 2 + (1 - c)
    x_up = ((x + 1) % NX) * NZ + z
    x_dn = ((x + 3) % NX) * NZ + z
    owner = z % 4 != 3
    beyond = ((x + 3 + 2 * c) % NX) * NZ + z
    edge = 3 * c

    weights = []
    for h in range(heads):
        weights.append(
            pltpu.make_async_copy(w_hbm.at[h, :, pl.ds(HD, 2 * HD)], wkv.at[h], wsem.at[h])
        )
    for h in range(heads):
        weights.append(
            pltpu.make_async_copy(
                w_hbm.at[h, :, pl.ds(0, HD)], wq.at[:, pl.ds(h * HD, HD)], wsem.at[heads + h]
            )
        )
    weights.append(pltpu.make_async_copy(wo_hbm, wo, wosem))
    for copy in weights:
        copy.start()

    peers = [(blk, mate), (blk, up), (blk, dn), (x_up, uly), (x_dn, uly), (beyond, mate)]
    for step in range(1, NZ):
        for core in (0, 1):
            peers.append((line + (z + step) % NZ, y * 2 + core))
    barrier = pltpu.get_barrier_semaphore()
    for to_blk, to_uly in peers:
        pl.semaphore_signal(
            barrier, inc=1, device_id={"blk": to_blk, "uly": to_uly}, device_id_type=MESH
        )

    values = x_ref[...].astype(jnp.float32)
    mean = jnp.mean(values, axis=-1, keepdims=True)
    centred = values - mean
    var = jnp.mean(centred * centred, axis=-1, keepdims=True)
    normed = centred * lax.rsqrt(var + 1e-06) * (1.0 + scale_ref[...]) + shift_ref[...]
    xbuf[pl.ds(pl.multiple_of(uly * rows, 16), rows), :] = normed.astype(xbuf.dtype)

    pl.semaphore_wait(barrier, len(peers))

    def piece(u, k):
        return xbuf.at[pl.ds(pl.multiple_of(u * rows, 16), rows), pl.ds(k * half, half)]

    gathered = []

    def spread(u, k, to):
        copy = push(piece(u, k), piece(u, k), gsem.at[len(gathered)], grsem.at[u, k], blk, to)
        copy.start()
        gathered.append(copy)

    def arrive(u, k):
        push(piece(u, k), piece(u, k), gsem.at[0], grsem.at[u, k], blk, mate).wait_recv()

    def chunk_rows(step):
        return pl.ds(pl.multiple_of(((y + step) % NY) * chunk, 16), chunk)

    def give(src, dst, send_sem, recv_sem, to_blk, to_uly, is_self):
        @pl.when(jnp.logical_not(is_self))
        def _():
            push(src, dst, send_sem, recv_sem, to_blk, to_uly).start()

        @pl.when(is_self)
        def _():
            pltpu.make_async_copy(src, dst, recv_sem).start()

    def given(src, dst, send_sem, recv_sem, to_blk, to_uly, is_self):
        @pl.when(jnp.logical_not(is_self))
        def _():
            push(src, dst, send_sem, recv_sem, to_blk, to_uly).wait_send()

    def turn(n):
        return (z + n) % heads

    def kv_out(n, step):
        h = turn(n)
        zd = 4 * c + h
        core = z % 2
        at = chunk_rows(step)
        return (
            stage.at[h, pl.ds(1, 2), at], kv.at[blk, :, at], asem.at[n, step],
            kvsem.at[blk, (y + step) % NY],
            line + zd, y * 2 + core, jnp.logical_and(zd == z, core == c),
        )

    def q_out(n, step):
        h = turn(n)
        zd = 4 * c + h
        core = z // 4
        at = chunk_rows(step)
        return (
            stage.at[h, 0, at], qb.at[z % 4, at], aqsem.at[n, step], qsem.at[z % 4],
            line + zd, y * 2 + core, jnp.logical_and(zd == z, core == c),
        )

    def project_queries(steps):
        left = jnp.concatenate([xbuf[chunk_rows(step), :] for step in steps], axis=0)
        result = jnp.dot(left, wq[...], preferred_element_type=jnp.float32)
        for h in range(heads):
            for n, step in enumerate(steps):
                stage[h, 0, chunk_rows(step), :] = result[
                    n * chunk : (n + 1) * chunk, h * HD : (h + 1) * HD
                ].astype(stage.dtype)
        for n in range(heads):
            for step in steps:
                give(*q_out(n, step))

    def project(steps):
        left = jnp.concatenate([xbuf[chunk_rows(step), :] for step in steps], axis=0)
        for h in range(heads):
            result = jnp.dot(left, wkv[h], preferred_element_type=jnp.float32)
            for n, step in enumerate(steps):
                for part in (0, 1):
                    stage[h, 1 + part, chunk_rows(step), :] = result[
                        n * chunk : (n + 1) * chunk, part * HD : (part + 1) * HD
                    ].astype(stage.dtype)
        for step in steps:
            for n in range(heads):
                give(*kv_out(n, step))

    odd = (z + c) % 2
    mine = []
    for even_gap, odd_gap in ((0, 1), (2, 7), (6, 3), (4, 5)):
        mine.append((z + even_gap + odd * (odd_gap - even_gap)) % NZ)
    X_UP, X_DN, MATE_LINE, MATE_BELOW, MATE_ABOVE, RELAY, MATE_ACROSS = range(7)

    def kv_part(slot, step):
        return kv.at[slot, :, chunk_rows(step)]

    def kv_wait(slot, step):
        ref = kv_part(slot, step)
        push(ref, ref, fsem.at[0], kvsem.at[slot, (y + step) % NY], blk, mate).wait_recv()

    def kv_pass(slot, step, kind, to_blk, to_uly, recv_sem):
        ref = kv_part(slot, step)
        push(ref, ref, fsem.at[kind], recv_sem, to_blk, to_uly).start()

    def pump_line(step):
        n = (y + step) % NY
        for zs in mine:
            slot = line + zs
            kv_wait(slot, step)
            kv_pass(slot, step, X_UP, x_up, uly, kvsem.at[slot, n])
            kv_pass(slot, step, X_DN, x_dn, uly, kvsem.at[slot, n])
            kv_pass(slot, step, MATE_LINE, blk, mate, matesem)

    def pump_sides(step):
        n = (y + step) % NY
        for zs in mine:
            below = ((x + 3) % NX) * NZ + zs
            above = ((x + 1) % NX) * NZ + zs
            kv_wait(below, step)
            kv_pass(below, step, MATE_BELOW, blk, mate, matesem)
            kv_wait(above, step)
            kv_pass(above, step, MATE_ABOVE, blk, mate, matesem)
        far = ((x + 1 + 2 * c) % NX) * NZ + 7 * c
        kv_pass(far, step, RELAY, beyond, uly, kvsem.at[far, n])

    def pump_across(step):
        across = ((x + 2) % NX) * NZ + 7 * c
        kv_wait(across, step)
        kv_pass(across, step, MATE_ACROSS, blk, mate, matesem)

    for first in (0, 1):
        spread(uly, first, up)
        spread(uly, 1 - first, dn)
        spread(uly, first, mate)
    for k in (0, 1):
        arrive(mate, k)
    for h in range(heads):
        weights[h].wait()
    project((0,))
    for h in range(heads):
        weights[heads + h].wait()
    project_queries((0,))

    def mate_of(u):
        return u + 1 - 2 * c

    arrive(dn, 0)
    spread(dn, 0, up)
    spread(dn, 0, mate)
    arrive(up, 1)
    spread(up, 1, dn)
    spread(up, 1, mate)
    arrive(dn, 1)
    spread(dn, 1, mate)
    arrive(up, 0)
    spread(up, 0, mate)
    for k in (0, 1):
        arrive(mate_of(dn), k)
        arrive(mate_of(up), k)
    project((3, 1))

    @pl.when(owner)
    def _():
        pump_line(0)

    arrive(opp, 0)
    spread(opp, 0, mate)
    arrive(opp, 1)
    spread(opp, 1, mate)
    for k in (0, 1):
        arrive(mate_of(opp), k)
    project((2,))
    project_queries((3, 1, 2))

    order = (2, 1, 3, 0)
    obs = (ob_first, ob_last)

    def o_out(which, i, n, src):
        core = z // 4
        h = z % 4
        to_z = 4 * c + i
        step = order[2 * which + n]
        return (
            src.at[pl.ds(n * chunk, chunk)], back.at[h, chunk_rows(step)],
            osem.at[which, i, n], bsem.at[h, (y + step) % NY],
            line + to_z, y * 2 + core, jnp.logical_and(to_z == z, core == c),
        )

    def q_trade():
        return push(qb.at[edge], qb.at[4], qxsem, qxrsem, beyond, mate)

    def o_trade(which):
        ob = obs[which]
        return push(ob.at[edge], ob.at[4], oxsem.at[which], oxrsem.at[which], beyond, mate)

    @pl.when(owner)
    def _():
        pump_line(3)
        pump_line(1)
        pump_sides(0)
        pump_line(2)
        pump_sides(3)
        pump_sides(1)
        pump_across(0)
        for i in range(4):
            push(qb.at[i], qb.at[i], fsem.at[0], qsem.at[i], blk, mate).wait_recv()
        q_trade().start()
        pump_sides(2)
        pump_across(3)
        pump_across(1)
        pump_across(2)
        rest = kv.at[pl.ds(0, 13)]
        push(rest, rest, fsem.at[0], matesem, blk, mate).wait_recv()
        q_trade().wait_recv()

        factor = 1.0 / (HD**0.5)
        end = line + 4 * c + edge
        swapped = jnp.clip((map_ref[end] - end) * (2 * c - 1), 0, 1)

        def attend(which):
            ob = obs[which]
            spans = [chunk_rows(step) for step in order[2 * which : 2 * which + 2]]

            def one_tile(n, _):
                inner = jnp.minimum(n, 1)
                i = (edge + inner * (1 + (n + 2 + z) % 3)) % 4
                other = (1 - inner) * swapped
                position = line + 4 * c + i + other * (2 * c - 1)
                row0 = corner_ref[0, position]
                col0 = corner_ref[1, position]
                at = i + other * (4 - i)
                queries = jnp.concatenate([qb[at, span, :] for span in spans], axis=0)
                slots = []
                best = None
                for w in range(WIN * WIN):
                    slot = map_ref[(row0 + w // WIN) * GW + col0 + w % WIN]
                    slots.append(slot)
                    s = lax.dot_general(
                        queries, kv[slot, 0], (((1,), (1,)), ((), ())),
                        preferred_element_type=jnp.float32,
                    )
                    scores[w] = s
                    for m in range(TILE // HD):
                        part = s[:, m * HD : (m + 1) * HD]
                        best = part if best is None else jnp.maximum(best, part)
                highest = jnp.max(best, axis=-1, keepdims=True)
                total = jnp.zeros((2 * chunk, HD), jnp.float32)
                accum = jnp.zeros((2 * chunk, HD), jnp.float32)
                for w in range(WIN * WIN):
                    probs = jnp.exp((scores[w] - highest) * factor)
                    for m in range(TILE // HD):
                        total = total + probs[:, m * HD : (m + 1) * HD]
                    accum = accum + jnp.dot(
                        probs.astype(jnp.bfloat16), kv[slots[w], 1],
                        preferred_element_type=jnp.float32,
                    )
                denom = jnp.sum(total, axis=-1, keepdims=True)
                ob[i] = (accum / denom).astype(ob.dtype)

                @pl.when(n == 0)
                def _():
                    o_trade(which).start()

                @pl.when(n > 0)
                def _():
                    for m in (0, 1):
                        give(*o_out(which, i, m, ob.at[i]))

                return 0

            lax.fori_loop(0, 4, one_tile, 0)
            o_trade(which).wait_recv()
            edge_out[which] = ob[edge + swapped * (4 - edge)]
            for m in (0, 1):
                give(*o_out(which, edge, m, edge_out.at[which]))

        attend(0)
        attend(1)

    weights[-1].wait()
    mates = []

    def out_block(n):
        step = order[n]
        for h in range(heads):
            ref = back.at[h, chunk_rows(step)]
            push(ref, ref, fsem.at[0], bsem.at[h, (y + step) % NY], blk, mate).wait_recv()
        for k, core in enumerate((1 - c, c)):
            u = ((y + step) % NY) * 2 + core
            for h in range(heads):
                lhs[n, pl.ds(k * rows, rows), pl.ds(h * HD, HD)] = back[
                    h, pl.ds(pl.multiple_of(u * rows, 16), rows), :
                ]
        part = jnp.dot(lhs[n], wo[...], preferred_element_type=jnp.float32)
        give_mate[n] = part[:rows].astype(give_mate.dtype)
        copy = push(give_mate.at[n], from_mate.at[n], msem.at[n], mrsem.at[n], blk, mate)
        copy.start()
        mates.append(copy)
        acc[n] = part[rows:]

    def cols(k):
        return slice(k * half, (k + 1) * half)

    def mixed(n, k):
        return acc[n, :, cols(k)] + from_mate[n, :, cols(k)].astype(jnp.float32)

    sent = []

    def relay(k, to):
        relay_out[k] = mixed(0, k).astype(relay_out.dtype)
        copy = push(relay_out.at[k], relay_in.at[k], ssem.at[k], rsem.at[k], blk, to)
        copy.start()
        sent.append(copy)

    def finish(d, k, to, extra):
        value = mixed(1 + d, k)
        if extra is not None:
            value = value + extra
        fin_out[d, k] = value.astype(fin_out.dtype)
        n = 2 + d * 2 + k
        copy = push(fin_out.at[d, k], fin_in.at[d, k], ssem.at[n], rsem.at[n], blk, to)
        copy.start()
        sent.append(copy)

    out_block(0)
    out_block(1)
    mates[0].wait_recv()
    relay(0, up)
    relay(1, dn)
    mates[1].wait_recv()
    finish(0, 1, up, None)
    out_block(2)
    mates[2].wait_recv()
    finish(1, 0, dn, None)
    for d, to in ((0, up), (1, dn)):
        sent[d].wait_recv()
        finish(d, d, to, relay_in[d].astype(jnp.float32))
    out_block(3)
    mates[3].wait_recv()
    for copy in sent[2:]:
        copy.wait_recv()
    for k in (0, 1):
        total = mixed(3, k) + fin_in[0, k].astype(jnp.float32) + fin_in[1, k].astype(jnp.float32)
        out_ref[:, cols(k)] = (gate_ref[:, cols(k)] * total).astype(out_ref.dtype)

    for copy in gathered + sent + mates:
        copy.wait_send()
    for n in range(heads):
        for step in range(NY):
            given(*kv_out(n, step))
            given(*q_out(n, step))

    @pl.when(owner)
    def _():
        q_trade().wait_send()
        for kind in range(7):
            tiles = 1 if kind in (RELAY, MATE_ACROSS) else 4
            ref = kv.at[pl.ds(0, tiles)]
            push(ref, ref, fsem.at[kind], matesem, blk, mate).wait_send()
        for which in (0, 1):
            o_trade(which).wait_send()
            for i in range(4):
                for m in (0, 1):
                    given(*o_out(which, i, m, edge_out.at[which]))


def vmem():
    return pl.BlockSpec(memory_space=pltpu.VMEM)


def hbm():
    return pl.BlockSpec(memory_space=pl.ANY)


def smem():
    return pl.BlockSpec(memory_space=pltpu.SMEM)


def on_device(tokens, mod_shift, mod_scale, out_gate, w_qkv, w_out, tile_map, window_corner):
    rows, width = tokens.shape
    heads = w_qkv.shape[1]
    bf16 = jnp.bfloat16
    f32 = jnp.float32
    dma = pltpu.SemaphoreType.DMA
    return pl.pallas_call(
        block_kernel,
        out_shape=jax.ShapeDtypeStruct((rows, width), bf16),
        in_specs=[smem(), smem(), vmem(), vmem(), vmem(), vmem(), hbm(), hbm()],
        out_specs=vmem(),
        scratch_shapes=[
            pltpu.VMEM((TILE, width), bf16),
            pltpu.VMEM((heads, width, 2 * HD), bf16),
            pltpu.VMEM((width, heads * HD), bf16),
            pltpu.VMEM((heads * HD, width), bf16),
            pltpu.VMEM((heads, 3, TILE, HD), bf16),
            pltpu.VMEM((NX * NZ, 2, TILE, HD), bf16),
            pltpu.VMEM((5, TILE, HD), bf16),
            pltpu.VMEM((5, TILE // 2, HD), bf16),
            pltpu.VMEM((5, TILE // 2, HD), bf16),
            pltpu.VMEM((2, TILE // 2, HD), bf16),
            pltpu.VMEM((heads, TILE, HD), bf16),
            pltpu.VMEM((WIN * WIN, TILE // 2, TILE), f32),
            pltpu.VMEM((4, 2 * rows, heads * HD), bf16),
            pltpu.VMEM((4, rows, width), f32),
            pltpu.VMEM((4, rows, width), bf16),
            pltpu.VMEM((4, rows, width), bf16),
            pltpu.VMEM((2, rows, width // 2), bf16),
            pltpu.VMEM((2, rows, width // 2), bf16),
            pltpu.VMEM((2, 2, rows, width // 2), bf16),
            pltpu.VMEM((2, 2, rows, width // 2), bf16),
            dma((6,)),
            dma,
            dma((14,)),
            dma((8, 2)),
            dma((3, 4)),
            dma((3, 4)),
            dma((NX * NZ, 4)),
            dma,
            dma((7,)),
            dma((4,)),
            dma((3, 4)),
            dma((2, 4, 2)),
            dma,
            dma,
            dma((2,)),
            dma((2,)),
            dma((4,)),
            dma((4,)),
            dma((6,)),
            dma((6,)),
        ],
        compiler_params=pltpu.CompilerParams(
            collective_id=0, has_side_effects=True, vmem_limit_bytes=VMEM_LIMIT
        ),
        name="block",
    )(
        tile_map, window_corner.T, tokens, mod_shift[None, :], mod_scale[None, :],
        out_gate[None, :], jnp.transpose(w_qkv, (1, 0, 2)), w_out,
    )


def solution(mesh):
    in_specs = (
        P(("blk", "uly"), None),
        P(),
        P(),
        P(),
        P(None, "uly", None),
        P("uly", None),
        P(),
        P(),
    )
    out_specs = P(("blk", "uly"), None)
    return jax.shard_map(
        on_device, mesh=mesh, in_specs=in_specs, out_specs=out_specs, check_vma=False
    )
```

```python
import jax
import jax.numpy as jnp
from jax import lax
from jax.experimental import pallas as pl
from jax.experimental.pallas import tpu as pltpu
from jax.sharding import PartitionSpec as P

TILE = 384
WIN = 3
GW = 4
NX = 4
NZ = 8
NY = 4
HD = 128
MESH = pl.DeviceIdType.MESH
VMEM_LIMIT = 62 * 1024 * 1024


def push(src, dst, send_sem, recv_sem, blk, uly):
    return pltpu.make_async_remote_copy(
        src_ref=src,
        dst_ref=dst,
        send_sem=send_sem,
        recv_sem=recv_sem,
        device_id={"blk": blk, "uly": uly},
        device_id_type=MESH,
    )


def block_kernel(
    map_ref, corner_ref, x_ref, shift_ref, scale_ref, gate_ref, w_hbm, wo_hbm, out_ref,
    xbuf, wkv, wq, wo, stage, kv, qb, ob, edge_in, edge_out, back, scores,
    lhs, acc, give_mate, from_mate, relay_out, relay_in, fin_out, fin_in,
    wsem, wosem, gsem, grsem, asem, aqsem, kvsem, matesem, fsem, qsem, bsem, osem,
    qxsem, qxrsem, oxsem, oxrsem, msem, mrsem, ssem, rsem,
):
    blk = lax.axis_index("blk")
    uly = lax.axis_index("uly")
    y, c = uly // 2, uly % 2
    x, z = blk // NZ, blk % NZ
    line = x * NZ
    rows, width = x_ref.shape
    half = width // 2
    chunk = 2 * rows
    heads = w_hbm.shape[0]
    up = ((y + 1) % NY) * 2 + c
    dn = ((y + 3) % NY) * 2 + c
    ahead = (y + 1 + 2 * c) % NY
    behind = (y + 3 + 2 * c) % NY
    onward = ahead * 2 + c
    mate = y * 2 + (1 - c)
    x_up = ((x + 1) % NX) * NZ + z
    x_dn = ((x + 3) % NX) * NZ + z
    x_far = ((x + 2) % NX) * NZ + z
    owner = z % 4 != 3
    beyond = ((x + 3 + 2 * c) % NX) * NZ + z
    edge = 3 * c

    weights = []
    for h in range(heads):
        weights.append(
            pltpu.make_async_copy(w_hbm.at[h, :, pl.ds(HD, 2 * HD)], wkv.at[h], wsem.at[h])
        )
    for h in range(heads):
        weights.append(
            pltpu.make_async_copy(
                w_hbm.at[h, :, pl.ds(0, HD)], wq.at[:, pl.ds(h * HD, HD)], wsem.at[heads + h]
            )
        )
    weights.append(pltpu.make_async_copy(wo_hbm, wo, wosem))
    for copy in weights:
        copy.start()

    peers = [(blk, mate), (blk, up), (blk, dn), (x_up, uly), (x_dn, uly), (x_far, uly), (beyond, mate)]
    for step in range(1, NZ):
        for core in (0, 1):
            peers.append((line + (z + step) % NZ, y * 2 + core))
    barrier = pltpu.get_barrier_semaphore()
    for to_blk, to_uly in peers:
        pl.semaphore_signal(
            barrier, inc=1, device_id={"blk": to_blk, "uly": to_uly}, device_id_type=MESH
        )

    values = x_ref[...].astype(jnp.float32)
    mean = jnp.mean(values, axis=-1, keepdims=True)
    centred = values - mean
    var = jnp.mean(centred * centred, axis=-1, keepdims=True)
    normed = centred * lax.rsqrt(var + 1e-06) * (1.0 + scale_ref[...]) + shift_ref[...]
    xbuf[pl.ds(pl.multiple_of(uly * rows, 16), rows), :] = normed.astype(xbuf.dtype)

    pl.semaphore_wait(barrier, len(peers))

    def piece(u, k):
        return xbuf.at[
            pl.ds(pl.multiple_of(u * rows, 16), rows), pl.ds(pl.multiple_of(k * half, 128), half)
        ]

    gathered = []

    def spread(u, k, to):
        copy = push(piece(u, k), piece(u, k), gsem.at[len(gathered)], grsem.at[u, k], blk, to)
        copy.start()
        gathered.append(copy)

    def arrive(u, k):
        push(piece(u, k), piece(u, k), gsem.at[0], grsem.at[u, k], blk, mate).wait_recv()

    def chunk_rows(step):
        return pl.ds(pl.multiple_of(((y + step) % NY) * chunk, 16), chunk)

    def blocks(stage_no):
        if stage_no in (0, 3):
            return [chunk_rows(2 if stage_no else 0)]
        return [
            pl.ds(pl.multiple_of(u * rows, 16), rows)
            for u in (((y + 3) % NY) * 2 + stage_no - 1, ((y + 1) % NY) * 2 + 2 - stage_no)
        ]

    def give(src, dst, send_sem, recv_sem, to_blk, to_uly, is_self):
        @pl.when(jnp.logical_not(is_self))
        def _():
            push(src, dst, send_sem, recv_sem, to_blk, to_uly).start()

        @pl.when(is_self)
        def _():
            pltpu.make_async_copy(src, dst, recv_sem).start()

    def given(src, dst, send_sem, recv_sem, to_blk, to_uly, is_self):
        @pl.when(jnp.logical_not(is_self))
        def _():
            push(src, dst, send_sem, recv_sem, to_blk, to_uly).wait_send()

    def turn(n):
        return (z + n) % heads

    def kv_out(n, stage_no, b):
        h = turn(n)
        zd = 4 * c + h
        core = z % 2
        at = blocks(stage_no)[b]
        return (
            stage.at[h, pl.ds(1, 2), at], kv.at[blk, :, at], asem.at[n, stage_no, b],
            kvsem.at[blk, stage_no],
            line + zd, y * 2 + core, jnp.logical_and(zd == z, core == c),
        )

    def q_out(n, stage_no, b):
        h = turn(n)
        zd = 4 * c + h
        core = z // 4
        at = blocks(stage_no)[b]
        return (
            stage.at[h, 0, at], qb.at[z % 4, at], aqsem.at[n, stage_no, b], qsem.at[z % 4],
            line + zd, y * 2 + core, jnp.logical_and(zd == z, core == c),
        )

    def gather_rows(spans):
        return jnp.concatenate([xbuf[span, :] for span in spans], axis=0)

    def project(stage_no):
        spans = blocks(stage_no)
        left = gather_rows(spans)
        for h in range(heads):
            result = jnp.dot(left, wkv[h], preferred_element_type=jnp.float32)
            for b, span in enumerate(spans):
                for part in (0, 1):
                    stage[h, 1 + part, span, :] = result[
                        b * span.size : (b + 1) * span.size, part * HD : (part + 1) * HD
                    ].astype(stage.dtype)
        for n in range(heads):
            for b in range(len(spans)):
                give(*kv_out(n, stage_no, b))

    def project_queries(stages):
        spans = [span for stage_no in stages for span in blocks(stage_no)]
        result = jnp.dot(gather_rows(spans), wq[...], preferred_element_type=jnp.float32)
        done = 0
        for span in spans:
            for h in range(heads):
                stage[h, 0, span, :] = result[
                    done : done + span.size, h * HD : (h + 1) * HD
                ].astype(stage.dtype)
            done += span.size
        for n in range(heads):
            for stage_no in stages:
                for b in range(len(blocks(stage_no))):
                    give(*q_out(n, stage_no, b))

    odd = (z + c) % 2
    mine = []
    for even_gap, odd_gap in ((0, 1), (2, 7), (6, 3), (4, 5)):
        mine.append((z + even_gap + odd * (odd_gap - even_gap)) % NZ)
    X_UP, X_DN, MATE_LINE, MATE_BELOW, MATE_ABOVE, FAR, MATE_ACROSS = range(7)

    def kv_wait(slot, stage_no):
        ref = kv.at[slot, :, chunk_rows(0)]
        push(ref, ref, fsem.at[0], kvsem.at[slot, stage_no], blk, mate).wait_recv()

    def kv_pass(slot, stage_no, kind, to_blk, to_uly, recv_sem):
        for at in blocks(stage_no):
            ref = kv.at[slot, :, at]
            push(ref, ref, fsem.at[kind], recv_sem, to_blk, to_uly).start()

    def pump_line(stage_no):
        for zs in mine:
            slot = line + zs
            kv_wait(slot, stage_no)
            kv_pass(slot, stage_no, X_UP, x_up, uly, kvsem.at[slot, stage_no])
            kv_pass(slot, stage_no, X_DN, x_dn, uly, kvsem.at[slot, stage_no])
            kv_pass(slot, stage_no, MATE_LINE, blk, mate, matesem)
        last = line + 7 * c
        kv_pass(last, stage_no, FAR, x_far, uly, kvsem.at[last, stage_no])

    def pump_sides(stage_no):
        for zs in mine:
            below = ((x + 3) % NX) * NZ + zs
            above = ((x + 1) % NX) * NZ + zs
            kv_wait(below, stage_no)
            kv_pass(below, stage_no, MATE_BELOW, blk, mate, matesem)
            kv_wait(above, stage_no)
            kv_pass(above, stage_no, MATE_ABOVE, blk, mate, matesem)

    def pump_across(stage_no):
        across = ((x + 2) % NX) * NZ + 7 * c
        kv_wait(across, stage_no)
        kv_pass(across, stage_no, MATE_ACROSS, blk, mate, matesem)

    for k in (c, 1 - c):
        spread(uly, k, onward)
        spread(uly, k, mate)
    for k in (c, 1 - c):
        arrive(mate, k)
        spread(mate, k, onward)
    for h in range(heads):
        weights[h].wait()
    project(0)
    for h in range(heads):
        weights[heads + h].wait()
    project_queries((0,))
    for stage_no, core in ((1, c), (2, 1 - c)):
        arrive(behind * 2 + core, c)
        spread(behind * 2 + core, c, onward)
        spread(behind * 2 + core, c, mate)
        arrive(behind * 2 + core, 1 - c)
        spread(behind * 2 + core, 1 - c, mate)
        for k in (1 - c, c):
            arrive(ahead * 2 + 1 - core, k)
        project(stage_no)

    @pl.when(owner)
    def _():
        pump_line(0)

    across = ((y + 2) % NY) * 2
    for core in (c, 1 - c):
        arrive(across + core, c)
        spread(across + core, c, mate)
    for core in (1 - c, c):
        arrive(across + core, 1 - c)
    project(3)
    project_queries((1, 2, 3))

    order = (2, 1, 3, 0)

    def o_out(which, i, n, src):
        core = z // 4
        h = z % 4
        to_z = 4 * c + i
        step = 2 + which if n == 0 else 1 - which + NY
        return (
            src.at[pl.ds(n * chunk, chunk)], back.at[h, chunk_rows(step)],
            osem.at[which, i, n], bsem.at[h, (y + step) % NY],
            line + to_z, y * 2 + core, jnp.logical_and(to_z == z, core == c),
        )

    def q_trade():
        return push(qb.at[edge], qb.at[4], qxsem, qxrsem, beyond, mate)

    def o_trade(which):
        return push(
            ob.at[which, edge], edge_in.at[which], oxsem.at[which], oxrsem.at[which], beyond, mate
        )

    @pl.when(owner)
    def _():
        pump_line(1)
        pump_sides(0)
        pump_line(2)
        pump_sides(1)
        pump_line(3)
        pump_sides(2)
        for i in range(4):
            push(qb.at[i], qb.at[i], fsem.at[0], qsem.at[i], blk, mate).wait_recv()
        q_trade().start()
        pump_sides(3)
        for stage_no in range(4):
            pump_across(stage_no)
        rest = kv.at[pl.ds(0, 13)]
        push(rest, rest, fsem.at[0], matesem, blk, mate).wait_recv()
        q_trade().wait_recv()

        factor = 1.0 / (HD**0.5)
        end = line + 4 * c + edge
        swapped = jnp.clip((map_ref[end] - end) * (2 * c - 1), 0, 1)

        def settle(which):
            o_trade(which).wait_recv()
            edge_out[which] = jnp.where(swapped > 0, edge_in[which], ob[which, edge])
            for m in (0, 1):
                give(*o_out(which, edge, m, edge_out.at[which]))

        def half_tile(turn_no, _):
            later = jnp.clip(turn_no - 1, 0, 1)
            which = jnp.clip(turn_no - 2, 0, 5) // 3 * later + turn_no * (1 - later)
            i = (edge + later * (1 + (turn_no + 1 + z) % 3)) % 4
            other = (1 - later) * swapped
            position = line + 4 * c + i + other * (2 * c - 1)
            row0 = corner_ref[0, position]
            col0 = corner_ref[1, position]
            at = i + other * (4 - i)
            queries = jnp.concatenate(
                [qb[at, chunk_rows(step), :] for step in (2 + which, 1 - which + NY)], axis=0
            )
            slots = []
            best = None
            for w in range(WIN * WIN):
                slot = map_ref[(row0 + w // WIN) * GW + col0 + w % WIN]
                slots.append(slot)
                s = lax.dot_general(
                    queries, kv[slot, 0], (((1,), (1,)), ((), ())),
                    preferred_element_type=jnp.float32,
                )
                scores[w] = s
                for m in range(TILE // HD):
                    part = s[:, m * HD : (m + 1) * HD]
                    best = part if best is None else jnp.maximum(best, part)
            highest = jnp.max(best, axis=-1, keepdims=True)
            total = jnp.zeros((2 * chunk, HD), jnp.float32)
            accum = jnp.zeros((2 * chunk, HD), jnp.float32)
            for w in range(WIN * WIN):
                probs = jnp.exp((scores[w] - highest) * factor)
                for m in range(TILE // HD):
                    total = total + probs[:, m * HD : (m + 1) * HD]
                accum = accum + jnp.dot(
                    probs.astype(jnp.bfloat16), kv[slots[w], 1],
                    preferred_element_type=jnp.float32,
                )
            denom = jnp.sum(total, axis=-1, keepdims=True)
            ob[which, i] = (accum / denom).astype(ob.dtype)

            @pl.when(turn_no < 2)
            def _():
                o_trade(which).start()

            @pl.when(turn_no > 1)
            def _():
                for m in (0, 1):
                    give(*o_out(which, i, m, ob.at[which, i]))

            @pl.when(turn_no == 4)
            def _():
                settle(0)

            return 0

        lax.fori_loop(0, 8, half_tile, 0)
        settle(1)

    weights[-1].wait()
    mates = []

    def out_block(n):
        step = order[n]
        for h in range(heads):
            ref = back.at[h, chunk_rows(step)]
            push(ref, ref, fsem.at[0], bsem.at[h, (y + step) % NY], blk, mate).wait_recv()
        for k, core in enumerate((1 - c, c)):
            u = ((y + step) % NY) * 2 + core
            for h in range(heads):
                lhs[n, pl.ds(k * rows, rows), pl.ds(h * HD, HD)] = back[
                    h, pl.ds(pl.multiple_of(u * rows, 16), rows), :
                ]
        part = jnp.dot(lhs[n], wo[...], preferred_element_type=jnp.float32)
        give_mate[n] = part[:rows].astype(give_mate.dtype)
        copy = push(give_mate.at[n], from_mate.at[n], msem.at[n], mrsem.at[n], blk, mate)
        copy.start()
        mates.append(copy)
        acc[n] = part[rows:]

    def cols(k):
        return slice(k * half, (k + 1) * half)

    def mixed(n, k):
        return acc[n, :, cols(k)] + from_mate[n, :, cols(k)].astype(jnp.float32)

    sent = []

    def relay(k, to):
        relay_out[k] = mixed(0, k).astype(relay_out.dtype)
        copy = push(relay_out.at[k], relay_in.at[k], ssem.at[k], rsem.at[k], blk, to)
        copy.start()
        sent.append(copy)

    def finish(d, k, to, extra):
        value = mixed(1 + d, k)
        if extra is not None:
            value = value + extra
        fin_out[d, k] = value.astype(fin_out.dtype)
        n = 2 + d * 2 + k
        copy = push(fin_out.at[d, k], fin_in.at[d, k], ssem.at[n], rsem.at[n], blk, to)
        copy.start()
        sent.append(copy)

    out_block(0)
    out_block(1)
    mates[0].wait_recv()
    relay(0, up)
    relay(1, dn)
    mates[1].wait_recv()
    finish(0, 1, up, None)
    out_block(2)
    mates[2].wait_recv()
    finish(1, 0, dn, None)
    for d, to in ((0, up), (1, dn)):
        sent[d].wait_recv()
        finish(d, d, to, relay_in[d].astype(jnp.float32))
    out_block(3)
    mates[3].wait_recv()
    for copy in sent[2:]:
        copy.wait_recv()
    for k in (0, 1):
        total = mixed(3, k) + fin_in[0, k].astype(jnp.float32) + fin_in[1, k].astype(jnp.float32)
        out_ref[:, cols(k)] = (gate_ref[:, cols(k)] * total).astype(out_ref.dtype)

    for copy in gathered + sent + mates:
        copy.wait_send()
    for n in range(heads):
        for stage_no in range(4):
            for b in range(len(blocks(stage_no))):
                given(*kv_out(n, stage_no, b))
                given(*q_out(n, stage_no, b))

    @pl.when(owner)
    def _():
        q_trade().wait_send()
        for kind in range(7):
            tiles = 1 if kind in (FAR, MATE_ACROSS) else 4
            ref = kv.at[pl.ds(0, tiles)]
            push(ref, ref, fsem.at[kind], matesem, blk, mate).wait_send()
        for which in (0, 1):
            o_trade(which).wait_send()
            for i in range(4):
                for m in (0, 1):
                    given(*o_out(which, i, m, edge_out.at[which]))


def vmem():
    return pl.BlockSpec(memory_space=pltpu.VMEM)


def hbm():
    return pl.BlockSpec(memory_space=pl.ANY)


def smem():
    return pl.BlockSpec(memory_space=pltpu.SMEM)


def on_device(tokens, mod_shift, mod_scale, out_gate, w_qkv, w_out, tile_map, window_corner):
    rows, width = tokens.shape
    heads = w_qkv.shape[1]
    bf16 = jnp.bfloat16
    f32 = jnp.float32
    dma = pltpu.SemaphoreType.DMA
    return pl.pallas_call(
        block_kernel,
        out_shape=jax.ShapeDtypeStruct((rows, width), bf16),
        in_specs=[smem(), smem(), vmem(), vmem(), vmem(), vmem(), hbm(), hbm()],
        out_specs=vmem(),
        scratch_shapes=[
            pltpu.VMEM((TILE, width), bf16),
            pltpu.VMEM((heads, width, 2 * HD), bf16),
            pltpu.VMEM((width, heads * HD), bf16),
            pltpu.VMEM((heads * HD, width), bf16),
            pltpu.VMEM((heads, 3, TILE, HD), bf16),
            pltpu.VMEM((NX * NZ, 2, TILE, HD), bf16),
            pltpu.VMEM((5, TILE, HD), bf16),
            pltpu.VMEM((2, 4, TILE // 2, HD), bf16),
            pltpu.VMEM((2, TILE // 2, HD), bf16),
            pltpu.VMEM((2, TILE // 2, HD), bf16),
            pltpu.VMEM((heads, TILE, HD), bf16),
            pltpu.VMEM((WIN * WIN, TILE // 2, TILE), f32),
            pltpu.VMEM((4, 2 * rows, heads * HD), bf16),
            pltpu.VMEM((4, rows, width), f32),
            pltpu.VMEM((4, rows, width), bf16),
            pltpu.VMEM((4, rows, width), bf16),
            pltpu.VMEM((2, rows, width // 2), bf16),
            pltpu.VMEM((2, rows, width // 2), bf16),
            pltpu.VMEM((2, 2, rows, width // 2), bf16),
            pltpu.VMEM((2, 2, rows, width // 2), bf16),
            dma((6,)),
            dma,
            dma((14,)),
            dma((8, 2)),
            dma((3, 4, 2)),
            dma((3, 4, 2)),
            dma((NX * NZ, 4)),
            dma,
            dma((7,)),
            dma((4,)),
            dma((3, 4)),
            dma((2, 4, 2)),
            dma,
            dma,
            dma((2,)),
            dma((2,)),
            dma((4,)),
            dma((4,)),
            dma((6,)),
            dma((6,)),
        ],
        compiler_params=pltpu.CompilerParams(
            collective_id=0, has_side_effects=True, vmem_limit_bytes=VMEM_LIMIT
        ),
        name="block",
    )(
        tile_map, window_corner.T, tokens, mod_shift[None, :], mod_scale[None, :],
        out_gate[None, :], jnp.transpose(w_qkv, (1, 0, 2)), w_out,
    )


def solution(mesh):
    in_specs = (
        P(("blk", "uly"), None),
        P(),
        P(),
        P(),
        P(None, "uly", None),
        P("uly", None),
        P(),
        P(),
    )
    out_specs = P(("blk", "uly"), None)
    return jax.shard_map(
        on_device, mesh=mesh, in_specs=in_specs, out_specs=out_specs, check_vma=False
    )
```

```python
import jax
import jax.numpy as jnp
from jax import lax
from jax.experimental import pallas as pl
from jax.experimental.pallas import tpu as pltpu
from jax.sharding import PartitionSpec as P

TILE = 384
WIN = 3
GW = 4
NX = 4
NZ = 8
NY = 4
HD = 128
MESH = pl.DeviceIdType.MESH
VMEM_LIMIT = 62 * 1024 * 1024


def push(src, dst, send_sem, recv_sem, blk, uly):
    return pltpu.make_async_remote_copy(
        src_ref=src,
        dst_ref=dst,
        send_sem=send_sem,
        recv_sem=recv_sem,
        device_id={"blk": blk, "uly": uly},
        device_id_type=MESH,
    )


def block_kernel(
    map_ref, corner_ref, x_ref, shift_ref, scale_ref, gate_ref, w_hbm, wo_hbm, out_ref,
    xbuf, wkv, wq, wo, stage, kv, qb, ob, edge_in, edge_out, back, scores,
    lhs, acc, give_mate, from_mate, relay_out, relay_in, fin_out, fin_in,
    wsem, wosem, gsem, grsem, asem, aqsem, kvsem, matesem, fsem, qsem, bsem, osem,
    qxsem, qxrsem, oxsem, oxrsem, msem, mrsem, ssem, rsem,
):
    blk = lax.axis_index("blk")
    uly = lax.axis_index("uly")
    y, c = uly // 2, uly % 2
    x, z = blk // NZ, blk % NZ
    line = x * NZ
    rows, width = x_ref.shape
    half = width // 2
    chunk = 2 * rows
    heads = w_hbm.shape[0]
    up = ((y + 1) % NY) * 2 + c
    dn = ((y + 3) % NY) * 2 + c
    ahead = (y + 1 + 2 * c) % NY
    behind = (y + 3 + 2 * c) % NY
    onward = ahead * 2 + c
    mate = y * 2 + (1 - c)
    x_up = ((x + 1) % NX) * NZ + z
    x_dn = ((x + 3) % NX) * NZ + z
    x_far = ((x + 2) % NX) * NZ + z
    owner = z % 4 != 3
    beyond = ((x + 3 + 2 * c) % NX) * NZ + z
    edge = 3 * c

    weights = []
    for h in range(heads):
        weights.append(
            pltpu.make_async_copy(w_hbm.at[h, :, pl.ds(HD, 2 * HD)], wkv.at[h], wsem.at[h])
        )
    for h in range(heads):
        weights.append(
            pltpu.make_async_copy(
                w_hbm.at[h, :, pl.ds(0, HD)], wq.at[:, pl.ds(h * HD, HD)], wsem.at[heads + h]
            )
        )
    weights.append(pltpu.make_async_copy(wo_hbm, wo, wosem))
    for copy in weights:
        copy.start()

    peers = [(blk, mate), (blk, up), (blk, dn), (x_up, uly), (x_dn, uly), (x_far, uly), (beyond, mate)]
    for step in range(1, NZ):
        for core in (0, 1):
            peers.append((line + (z + step) % NZ, y * 2 + core))
    barrier = pltpu.get_barrier_semaphore()
    for to_blk, to_uly in peers:
        pl.semaphore_signal(
            barrier, inc=1, device_id={"blk": to_blk, "uly": to_uly}, device_id_type=MESH
        )

    values = x_ref[...].astype(jnp.float32)
    mean = jnp.mean(values, axis=-1, keepdims=True)
    centred = values - mean
    var = jnp.mean(centred * centred, axis=-1, keepdims=True)
    normed = centred * lax.rsqrt(var + 1e-06) * (1.0 + scale_ref[...]) + shift_ref[...]
    xbuf[pl.ds(pl.multiple_of(uly * rows, 16), rows), :] = normed.astype(xbuf.dtype)

    pl.semaphore_wait(barrier, len(peers))

    def piece(u, k):
        return xbuf.at[
            pl.ds(pl.multiple_of(u * rows, 16), rows), pl.ds(pl.multiple_of(k * half, 128), half)
        ]

    gathered = []

    def spread(u, k, to):
        copy = push(piece(u, k), piece(u, k), gsem.at[len(gathered)], grsem.at[u, k], blk, to)
        copy.start()
        gathered.append(copy)

    def arrive(u, k):
        push(piece(u, k), piece(u, k), gsem.at[0], grsem.at[u, k], blk, mate).wait_recv()

    def chunk_rows(step):
        return pl.ds(pl.multiple_of(((y + step) % NY) * chunk, 16), chunk)

    def blocks(stage_no):
        if stage_no in (0, 3):
            return [chunk_rows(2 if stage_no else 0)]
        return [
            pl.ds(pl.multiple_of(u * rows, 16), rows)
            for u in (((y + 3) % NY) * 2 + stage_no - 1, ((y + 1) % NY) * 2 + 2 - stage_no)
        ]

    def give(src, dst, send_sem, recv_sem, to_blk, to_uly, is_self):
        @pl.when(jnp.logical_not(is_self))
        def _():
            push(src, dst, send_sem, recv_sem, to_blk, to_uly).start()

        @pl.when(is_self)
        def _():
            pltpu.make_async_copy(src, dst, recv_sem).start()

    def given(src, dst, send_sem, recv_sem, to_blk, to_uly, is_self):
        @pl.when(jnp.logical_not(is_self))
        def _():
            push(src, dst, send_sem, recv_sem, to_blk, to_uly).wait_send()

    def turn(n):
        return (z + n) % heads

    def kv_out(n, stage_no, b):
        h = turn(n)
        zd = 4 * c + h
        core = z % 2
        at = blocks(stage_no)[b]
        return (
            stage.at[h, pl.ds(1, 2), at], kv.at[blk, :, at], asem.at[n, stage_no, b],
            kvsem.at[blk, stage_no],
            line + zd, y * 2 + core, jnp.logical_and(zd == z, core == c),
        )

    def q_out(n, stage_no, b):
        h = turn(n)
        zd = 4 * c + h
        core = z // 4
        at = blocks(stage_no)[b]
        return (
            stage.at[h, 0, at], qb.at[z % 4, at], aqsem.at[n, stage_no, b], qsem.at[z % 4],
            line + zd, y * 2 + core, jnp.logical_and(zd == z, core == c),
        )

    def gather_rows(spans):
        return jnp.concatenate([xbuf[span, :] for span in spans], axis=0)

    def project(stage_no):
        spans = blocks(stage_no)
        left = gather_rows(spans)
        for h in range(heads):
            result = jnp.dot(left, wkv[h], preferred_element_type=jnp.float32)
            for b, span in enumerate(spans):
                for part in (0, 1):
                    stage[h, 1 + part, span, :] = result[
                        b * span.size : (b + 1) * span.size, part * HD : (part + 1) * HD
                    ].astype(stage.dtype)
        for n in range(heads):
            for b in range(len(spans)):
                give(*kv_out(n, stage_no, b))

    def project_queries(stages):
        spans = [span for stage_no in stages for span in blocks(stage_no)]
        result = jnp.dot(gather_rows(spans), wq[...], preferred_element_type=jnp.float32)
        done = 0
        for span in spans:
            for h in range(heads):
                stage[h, 0, span, :] = result[
                    done : done + span.size, h * HD : (h + 1) * HD
                ].astype(stage.dtype)
            done += span.size
        for n in range(heads):
            for stage_no in stages:
                for b in range(len(blocks(stage_no))):
                    give(*q_out(n, stage_no, b))

    odd = (z + c) % 2
    mine = []
    for even_gap, odd_gap in ((0, 1), (2, 7), (6, 3), (4, 5)):
        mine.append((z + even_gap + odd * (odd_gap - even_gap)) % NZ)
    X_UP, X_DN, MATE_LINE, MATE_BELOW, MATE_ABOVE, FAR, MATE_ACROSS = range(7)

    def kv_wait(slot, stage_no):
        ref = kv.at[slot, :, chunk_rows(0)]
        push(ref, ref, fsem.at[0], kvsem.at[slot, stage_no], blk, mate).wait_recv()

    def kv_pass(slot, stage_no, kind, to_blk, to_uly, recv_sem):
        for at in blocks(stage_no):
            ref = kv.at[slot, :, at]
            push(ref, ref, fsem.at[kind], recv_sem, to_blk, to_uly).start()

    def pump_line(stage_no):
        for zs in mine:
            slot = line + zs
            kv_wait(slot, stage_no)
            kv_pass(slot, stage_no, X_UP, x_up, uly, kvsem.at[slot, stage_no])
            kv_pass(slot, stage_no, X_DN, x_dn, uly, kvsem.at[slot, stage_no])
            kv_pass(slot, stage_no, MATE_LINE, blk, mate, matesem)
        if stage_no == 3:
            last = line + 7 * c
            kv_pass(last, stage_no, FAR, x_far, uly, kvsem.at[last, stage_no])

    def pump_sides(stage_no):
        for zs in mine:
            below = ((x + 3) % NX) * NZ + zs
            above = ((x + 1) % NX) * NZ + zs
            kv_wait(below, stage_no)
            kv_pass(below, stage_no, MATE_BELOW, blk, mate, matesem)
            kv_wait(above, stage_no)
            kv_pass(above, stage_no, MATE_ABOVE, blk, mate, matesem)
        if stage_no < 3:
            last = ((x + 1 + 2 * c) % NX) * NZ + 7 * c
            kv_pass(last, stage_no, FAR, beyond, uly, kvsem.at[last, stage_no])

    def pump_across(stage_no):
        across = ((x + 2) % NX) * NZ + 7 * c
        kv_wait(across, stage_no)
        kv_pass(across, stage_no, MATE_ACROSS, blk, mate, matesem)

    for k in (c, 1 - c):
        spread(uly, k, onward)
        spread(uly, k, mate)
    for k in (c, 1 - c):
        arrive(mate, k)
        spread(mate, k, onward)
    for h in range(heads):
        weights[h].wait()
    project(0)
    for h in range(heads):
        weights[heads + h].wait()
    project_queries((0,))
    for stage_no, core in ((1, c), (2, 1 - c)):
        arrive(behind * 2 + core, c)
        spread(behind * 2 + core, c, onward)
        spread(behind * 2 + core, c, mate)
        arrive(behind * 2 + core, 1 - c)
        spread(behind * 2 + core, 1 - c, mate)
        for k in (1 - c, c):
            arrive(ahead * 2 + 1 - core, k)
        project(stage_no)

    @pl.when(owner)
    def _():
        pump_line(0)

    across = ((y + 2) % NY) * 2
    for core in (c, 1 - c):
        arrive(across + core, c)
        spread(across + core, c, mate)
    for core in (1 - c, c):
        arrive(across + core, 1 - c)
    project(3)
    project_queries((1, 2, 3))

    order = (2, 1, 3, 0)

    def step_of(g):
        if isinstance(g, int):
            return order[g]
        return jnp.where(g == 0, 2, jnp.where(g == 1, 1, jnp.where(g == 2, 3, 0)))


    def o_out(g, i, src):
        core = z // 4
        h = z % 4
        to_z = 4 * c + i
        step = step_of(g)
        return (
            src, back.at[h, chunk_rows(step)], osem.at[g, i], bsem.at[h, (y + step) % NY],
            line + to_z, y * 2 + core, jnp.logical_and(to_z == z, core == c),
        )

    def q_trade():
        return push(qb.at[edge], qb.at[4], qxsem, qxrsem, beyond, mate)

    def o_trade(g):
        return push(ob.at[g, edge], edge_in.at[g], oxsem.at[g], oxrsem.at[g], beyond, mate)

    @pl.when(owner)
    def _():
        pump_line(1)
        pump_sides(0)
        pump_line(2)
        pump_sides(1)
        pump_line(3)
        pump_sides(2)
        for i in range(4):
            push(qb.at[i], qb.at[i], fsem.at[0], qsem.at[i], blk, mate).wait_recv()
        q_trade().start()
        pump_sides(3)
        for stage_no in range(4):
            pump_across(stage_no)
        rest = kv.at[pl.ds(0, 13)]
        push(rest, rest, fsem.at[0], matesem, blk, mate).wait_recv()
        q_trade().wait_recv()

        factor = 1.0 / (HD**0.5)
        end = line + 4 * c + edge
        swapped = jnp.clip((map_ref[end] - end) * (2 * c - 1), 0, 1)

        def settle(g):
            o_trade(g).wait_recv()
            edge_out[g] = jnp.where(swapped > 0, edge_in[g], ob[g, edge])
            give(*o_out(g, edge, edge_out.at[g]))

        def quarter_tile(turn_no, _):
            past = jnp.maximum(turn_no - 1, 0)
            r = past % 4
            full = past // 4
            ends = jnp.logical_or(turn_no == 0, jnp.logical_and(r == 1, full < 3))
            g = jnp.where(turn_no == 0, 0, jnp.where(ends, full + 1, full))
            n = jnp.where(full == 3, r, jnp.where(r == 0, 0, r - 1))
            i = jnp.where(ends, edge, (edge + 1 + (n + z) % 3) % 4)
            other = jnp.where(ends, 1, 0) * swapped
            position = line + 4 * c + i + other * (2 * c - 1)
            row0 = corner_ref[0, position]
            col0 = corner_ref[1, position]
            queries = qb[i + other * (4 - i), chunk_rows(step_of(g)), :]
            slots = []
            best = None
            for w in range(WIN * WIN):
                slot = map_ref[(row0 + w // WIN) * GW + col0 + w % WIN]
                slots.append(slot)
                s = lax.dot_general(
                    queries, kv[slot, 0], (((1,), (1,)), ((), ())),
                    preferred_element_type=jnp.float32,
                )
                scores[w] = s
                for m in range(TILE // HD):
                    part = s[:, m * HD : (m + 1) * HD]
                    best = part if best is None else jnp.maximum(best, part)
            highest = jnp.max(best, axis=-1, keepdims=True)
            total = jnp.zeros((chunk, HD), jnp.float32)
            accum = jnp.zeros((chunk, HD), jnp.float32)
            for w in range(WIN * WIN):
                probs = jnp.exp((scores[w] - highest) * factor)
                for m in range(TILE // HD):
                    total = total + probs[:, m * HD : (m + 1) * HD]
                accum = accum + jnp.dot(
                    probs.astype(jnp.bfloat16), kv[slots[w], 1],
                    preferred_element_type=jnp.float32,
                )
            denom = jnp.sum(total, axis=-1, keepdims=True)
            ob[g, i] = (accum / denom).astype(ob.dtype)

            @pl.when(ends)
            def _():
                o_trade(g).start()

            @pl.when(jnp.logical_not(ends))
            def _():
                give(*o_out(g, i, ob.at[g, i]))

            for done in range(3):

                @pl.when(turn_no == 4 * done + 4)
                def _():
                    settle(done)

            return 0

        lax.fori_loop(0, 16, quarter_tile, 0)
        settle(3)

    weights[-1].wait()
    mates = []

    def out_block(n):
        step = order[n]
        for h in range(heads):
            ref = back.at[h, chunk_rows(step)]
            push(ref, ref, fsem.at[0], bsem.at[h, (y + step) % NY], blk, mate).wait_recv()
        for k, core in enumerate((1 - c, c)):
            u = ((y + step) % NY) * 2 + core
            for h in range(heads):
                lhs[n, pl.ds(k * rows, rows), pl.ds(h * HD, HD)] = back[
                    h, pl.ds(pl.multiple_of(u * rows, 16), rows), :
                ]
        part = jnp.dot(lhs[n], wo[...], preferred_element_type=jnp.float32)
        give_mate[n] = part[:rows].astype(give_mate.dtype)
        copy = push(give_mate.at[n], from_mate.at[n], msem.at[n], mrsem.at[n], blk, mate)
        copy.start()
        mates.append(copy)
        acc[n] = part[rows:]

    def cols(k):
        return slice(k * half, (k + 1) * half)

    def mixed(n, k):
        return acc[n, :, cols(k)] + from_mate[n, :, cols(k)].astype(jnp.float32)

    sent = []

    def relay(k, to):
        relay_out[k] = mixed(0, k).astype(relay_out.dtype)
        copy = push(relay_out.at[k], relay_in.at[k], ssem.at[k], rsem.at[k], blk, to)
        copy.start()
        sent.append(copy)

    def finish(d, k, to, extra):
        value = mixed(1 + d, k)
        if extra is not None:
            value = value + extra
        fin_out[d, k] = value.astype(fin_out.dtype)
        n = 2 + d * 2 + k
        copy = push(fin_out.at[d, k], fin_in.at[d, k], ssem.at[n], rsem.at[n], blk, to)
        copy.start()
        sent.append(copy)

    out_block(0)
    mates[0].wait_recv()
    relay(0, up)
    relay(1, dn)
    out_block(1)
    mates[1].wait_recv()
    finish(0, 1, up, None)
    out_block(2)
    mates[2].wait_recv()
    finish(1, 0, dn, None)
    for d, to in ((0, up), (1, dn)):
        sent[d].wait_recv()
        finish(d, d, to, relay_in[d].astype(jnp.float32))
    out_block(3)
    mates[3].wait_recv()
    for copy in sent[2:]:
        copy.wait_recv()
    for k in (0, 1):
        total = mixed(3, k) + fin_in[0, k].astype(jnp.float32) + fin_in[1, k].astype(jnp.float32)
        out_ref[:, cols(k)] = (gate_ref[:, cols(k)] * total).astype(out_ref.dtype)

    for copy in gathered + sent + mates:
        copy.wait_send()
    for n in range(heads):
        for stage_no in range(4):
            for b in range(len(blocks(stage_no))):
                given(*kv_out(n, stage_no, b))
                given(*q_out(n, stage_no, b))

    @pl.when(owner)
    def _():
        q_trade().wait_send()
        for kind in range(7):
            tiles = 1 if kind in (FAR, MATE_ACROSS) else 4
            ref = kv.at[pl.ds(0, tiles)]
            push(ref, ref, fsem.at[kind], matesem, blk, mate).wait_send()
        for g in range(4):
            o_trade(g).wait_send()
            for i in range(4):
                given(*o_out(g, i, edge_out.at[g]))


def vmem():
    return pl.BlockSpec(memory_space=pltpu.VMEM)


def hbm():
    return pl.BlockSpec(memory_space=pl.ANY)


def smem():
    return pl.BlockSpec(memory_space=pltpu.SMEM)


def on_device(tokens, mod_shift, mod_scale, out_gate, w_qkv, w_out, tile_map, window_corner):
    rows, width = tokens.shape
    heads = w_qkv.shape[1]
    bf16 = jnp.bfloat16
    f32 = jnp.float32
    dma = pltpu.SemaphoreType.DMA
    return pl.pallas_call(
        block_kernel,
        out_shape=jax.ShapeDtypeStruct((rows, width), bf16),
        in_specs=[smem(), smem(), vmem(), vmem(), vmem(), vmem(), hbm(), hbm()],
        out_specs=vmem(),
        scratch_shapes=[
            pltpu.VMEM((TILE, width), bf16),
            pltpu.VMEM((heads, width, 2 * HD), bf16),
            pltpu.VMEM((width, heads * HD), bf16),
            pltpu.VMEM((heads * HD, width), bf16),
            pltpu.VMEM((heads, 3, TILE, HD), bf16),
            pltpu.VMEM((NX * NZ, 2, TILE, HD), bf16),
            pltpu.VMEM((5, TILE, HD), bf16),
            pltpu.VMEM((4, 4, 2 * rows, HD), bf16),
            pltpu.VMEM((4, 2 * rows, HD), bf16),
            pltpu.VMEM((4, 2 * rows, HD), bf16),
            pltpu.VMEM((heads, TILE, HD), bf16),
            pltpu.VMEM((WIN * WIN, 2 * rows, TILE), f32),
            pltpu.VMEM((4, 2 * rows, heads * HD), bf16),
            pltpu.VMEM((4, rows, width), f32),
            pltpu.VMEM((4, rows, width), bf16),
            pltpu.VMEM((4, rows, width), bf16),
            pltpu.VMEM((2, rows, width // 2), bf16),
            pltpu.VMEM((2, rows, width // 2), bf16),
            pltpu.VMEM((2, 2, rows, width // 2), bf16),
            pltpu.VMEM((2, 2, rows, width // 2), bf16),
            dma((6,)),
            dma,
            dma((14,)),
            dma((8, 2)),
            dma((3, 4, 2)),
            dma((3, 4, 2)),
            dma((NX * NZ, 4)),
            dma,
            dma((7,)),
            dma((4,)),
            dma((3, 4)),
            dma((4, 4)),
            dma,
            dma,
            dma((4,)),
            dma((4,)),
            dma((4,)),
            dma((4,)),
            dma((6,)),
            dma((6,)),
        ],
        compiler_params=pltpu.CompilerParams(
            collective_id=0, has_side_effects=True, vmem_limit_bytes=VMEM_LIMIT
        ),
        name="block",
    )(
        tile_map, window_corner.T, tokens, mod_shift[None, :], mod_scale[None, :],
        out_gate[None, :], jnp.transpose(w_qkv, (1, 0, 2)), w_out,
    )


def solution(mesh):
    in_specs = (
        P(("blk", "uly"), None),
        P(),
        P(),
        P(),
        P(None, "uly", None),
        P("uly", None),
        P(),
        P(),
    )
    out_specs = P(("blk", "uly"), None)
    return jax.shard_map(
        on_device, mesh=mesh, in_specs=in_specs, out_specs=out_specs, check_vma=False
    )
```

```python
import jax
import jax.numpy as jnp
from jax import lax
from jax.experimental import pallas as pl
from jax.experimental.pallas import tpu as pltpu
from jax.sharding import PartitionSpec as P

TILE = 384
WIN = 3
GW = 4
NX = 4
NZ = 8
NY = 4
HD = 128
MESH = pl.DeviceIdType.MESH
VMEM_LIMIT = 62 * 1024 * 1024


def push(src, dst, send_sem, recv_sem, blk, uly):
    return pltpu.make_async_remote_copy(
        src_ref=src,
        dst_ref=dst,
        send_sem=send_sem,
        recv_sem=recv_sem,
        device_id={"blk": blk, "uly": uly},
        device_id_type=MESH,
    )


def block_kernel(
    map_ref, corner_ref, x_ref, shift_ref, scale_ref, gate_ref, w_hbm, wo_hbm, out_ref,
    xbuf, wkv, wq, wo, stage, kv, qb, q_in, q_now, ob, edge_in, edge_out, back, scores,
    lhs, acc, give_mate, from_mate, relay_out, relay_in, fin_out, fin_in,
    wsem, wosem, gsem, grsem, asem, aqsem, kvsem, matesem, fsem, qsem, bsem, osem,
    qxsem, qxrsem, oxsem, oxrsem, msem, mrsem, ssem, rsem,
):
    blk = lax.axis_index("blk")
    uly = lax.axis_index("uly")
    y, c = uly // 2, uly % 2
    x, z = blk // NZ, blk % NZ
    line = x * NZ
    rows, width = x_ref.shape
    half = width // 2
    chunk = 2 * rows
    heads = w_hbm.shape[0]
    up = ((y + 1) % NY) * 2 + c
    dn = ((y + 3) % NY) * 2 + c
    ahead = (y + 1 + 2 * c) % NY
    behind = (y + 3 + 2 * c) % NY
    onward = ahead * 2 + c
    mate = y * 2 + (1 - c)
    x_up = ((x + 1) % NX) * NZ + z
    x_dn = ((x + 3) % NX) * NZ + z
    x_far = ((x + 2) % NX) * NZ + z
    owner = z % 4 != 3
    beyond = ((x + 3 + 2 * c) % NX) * NZ + z
    edge = 3 * c

    weights = []
    for h in range(heads):
        weights.append(
            pltpu.make_async_copy(w_hbm.at[h, :, pl.ds(HD, 2 * HD)], wkv.at[h], wsem.at[h])
        )
    for h in range(heads):
        weights.append(
            pltpu.make_async_copy(
                w_hbm.at[h, :, pl.ds(0, HD)], wq.at[:, pl.ds(h * HD, HD)], wsem.at[heads + h]
            )
        )
    weights.append(pltpu.make_async_copy(wo_hbm, wo, wosem))
    for copy in weights:
        copy.start()

    peers = [(blk, mate), (blk, up), (blk, dn), (x_up, uly), (x_dn, uly), (x_far, uly), (beyond, mate)]
    for step in range(1, NZ):
        for core in (0, 1):
            peers.append((line + (z + step) % NZ, y * 2 + core))
    barrier = pltpu.get_barrier_semaphore()
    for to_blk, to_uly in peers:
        pl.semaphore_signal(
            barrier, inc=1, device_id={"blk": to_blk, "uly": to_uly}, device_id_type=MESH
        )

    values = x_ref[...].astype(jnp.float32)
    mean = jnp.mean(values, axis=-1, keepdims=True)
    centred = values - mean
    var = jnp.mean(centred * centred, axis=-1, keepdims=True)
    normed = centred * lax.rsqrt(var + 1e-06) * (1.0 + scale_ref[...]) + shift_ref[...]
    xbuf[pl.ds(pl.multiple_of(uly * rows, 16), rows), :] = normed.astype(xbuf.dtype)

    pl.semaphore_wait(barrier, len(peers))

    def piece(u, k):
        return xbuf.at[
            pl.ds(pl.multiple_of(u * rows, 16), rows), pl.ds(pl.multiple_of(k * half, 128), half)
        ]

    gathered = []

    def spread(u, k, to):
        copy = push(piece(u, k), piece(u, k), gsem.at[len(gathered)], grsem.at[u, k], blk, to)
        copy.start()
        gathered.append(copy)

    def arrive(u, k):
        push(piece(u, k), piece(u, k), gsem.at[0], grsem.at[u, k], blk, mate).wait_recv()

    def chunk_rows(step):
        return pl.ds(pl.multiple_of(((y + step) % NY) * chunk, 16), chunk)

    def blocks(stage_no):
        if stage_no in (0, 3):
            return [chunk_rows(2 if stage_no else 0)]
        return [
            pl.ds(pl.multiple_of(u * rows, 16), rows)
            for u in (((y + 3) % NY) * 2 + stage_no - 1, ((y + 1) % NY) * 2 + 2 - stage_no)
        ]

    def give(src, dst, send_sem, recv_sem, to_blk, to_uly, is_self):
        @pl.when(jnp.logical_not(is_self))
        def _():
            push(src, dst, send_sem, recv_sem, to_blk, to_uly).start()

        @pl.when(is_self)
        def _():
            pltpu.make_async_copy(src, dst, recv_sem).start()

    def given(src, dst, send_sem, recv_sem, to_blk, to_uly, is_self):
        @pl.when(jnp.logical_not(is_self))
        def _():
            push(src, dst, send_sem, recv_sem, to_blk, to_uly).wait_send()

    def turn(n):
        return (z + n) % heads

    def kv_out(n, stage_no, b):
        h = turn(n)
        zd = 4 * c + h
        core = z % 2
        at = blocks(stage_no)[b]
        return (
            stage.at[h, pl.ds(1, 2), at], kv.at[blk, :, at], asem.at[n, stage_no, b],
            kvsem.at[blk, stage_no],
            line + zd, y * 2 + core, jnp.logical_and(zd == z, core == c),
        )

    def q_out(n, stage_no, b):
        h = turn(n)
        zd = 4 * c + h
        core = z // 4
        at = blocks(stage_no)[b]
        return (
            stage.at[h, 0, at], qb.at[z % 4, at], aqsem.at[n, stage_no, b], qsem.at[z % 4],
            line + zd, y * 2 + core, jnp.logical_and(zd == z, core == c),
        )

    def gather_rows(spans):
        return jnp.concatenate([xbuf[span, :] for span in spans], axis=0)

    def project(stage_no):
        spans = blocks(stage_no)
        left = gather_rows(spans)
        for h in range(heads):
            result = jnp.dot(left, wkv[h], preferred_element_type=jnp.float32)
            for b, span in enumerate(spans):
                for part in (0, 1):
                    stage[h, 1 + part, span, :] = result[
                        b * span.size : (b + 1) * span.size, part * HD : (part + 1) * HD
                    ].astype(stage.dtype)
        for n in range(heads):
            for b in range(len(spans)):
                give(*kv_out(n, stage_no, b))

    def project_queries(stages):
        spans = [span for stage_no in stages for span in blocks(stage_no)]
        result = jnp.dot(gather_rows(spans), wq[...], preferred_element_type=jnp.float32)
        done = 0
        for span in spans:
            for h in range(heads):
                stage[h, 0, span, :] = result[
                    done : done + span.size, h * HD : (h + 1) * HD
                ].astype(stage.dtype)
            done += span.size
        for n in range(heads):
            for stage_no in stages:
                for b in range(len(blocks(stage_no))):
                    give(*q_out(n, stage_no, b))

    odd = (z + c) % 2
    mine = []
    for even_gap, odd_gap in ((0, 1), (2, 7), (6, 3), (4, 5)):
        mine.append((z + even_gap + odd * (odd_gap - even_gap)) % NZ)
    X_UP, X_DN, MATE_LINE, MATE_BELOW, MATE_ABOVE, FAR, MATE_ACROSS = range(7)

    def kv_wait(slot, stage_no):
        ref = kv.at[slot, :, chunk_rows(0)]
        push(ref, ref, fsem.at[0], kvsem.at[slot, stage_no], blk, mate).wait_recv()

    def kv_pass(slot, stage_no, kind, to_blk, to_uly, recv_sem):
        for at in blocks(stage_no):
            ref = kv.at[slot, :, at]
            push(ref, ref, fsem.at[kind], recv_sem, to_blk, to_uly).start()

    def pump_line(stage_no):
        for zs in mine:
            slot = line + zs
            kv_wait(slot, stage_no)
            kv_pass(slot, stage_no, X_UP, x_up, uly, kvsem.at[slot, stage_no])
            kv_pass(slot, stage_no, X_DN, x_dn, uly, kvsem.at[slot, stage_no])
            kv_pass(slot, stage_no, MATE_LINE, blk, mate, matesem)
        if stage_no == 3:
            last = line + 7 * c
            kv_pass(last, stage_no, FAR, x_far, uly, kvsem.at[last, stage_no])

    def pump_sides(stage_no):
        for zs in mine:
            below = ((x + 3) % NX) * NZ + zs
            above = ((x + 1) % NX) * NZ + zs
            kv_wait(below, stage_no)
            kv_pass(below, stage_no, MATE_BELOW, blk, mate, matesem)
            kv_wait(above, stage_no)
            kv_pass(above, stage_no, MATE_ABOVE, blk, mate, matesem)
        if stage_no < 3:
            last = ((x + 1 + 2 * c) % NX) * NZ + 7 * c
            kv_pass(last, stage_no, FAR, beyond, uly, kvsem.at[last, stage_no])

    def pump_across(stage_no):
        across = ((x + 2) % NX) * NZ + 7 * c
        kv_wait(across, stage_no)
        kv_pass(across, stage_no, MATE_ACROSS, blk, mate, matesem)

    for k in (c, 1 - c):
        spread(uly, k, onward)
        spread(uly, k, mate)
    for k in (c, 1 - c):
        arrive(mate, k)
        spread(mate, k, onward)
    for h in range(heads):
        weights[h].wait()
    project(0)
    for h in range(heads):
        weights[heads + h].wait()
    project_queries((0,))
    for stage_no, core in ((1, c), (2, 1 - c)):
        arrive(behind * 2 + core, c)
        spread(behind * 2 + core, c, onward)
        spread(behind * 2 + core, c, mate)
        arrive(behind * 2 + core, 1 - c)
        spread(behind * 2 + core, 1 - c, mate)
        for k in (1 - c, c):
            arrive(ahead * 2 + 1 - core, k)
        project(stage_no)

    @pl.when(owner)
    def _():
        pump_line(0)

    across = ((y + 2) % NY) * 2
    for core in (c, 1 - c):
        arrive(across + core, c)
        spread(across + core, c, mate)
    for core in (1 - c, c):
        arrive(across + core, 1 - c)
    project(3)

    @pl.when(owner)
    def _():
        pump_line(1)

    project_queries((1, 2, 3))

    order = (2, 1, 3, 0)

    def step_of(g, m):
        return 2 + g if m == 0 else 1 - g + NY

    def o_out(g, i, m, src):
        core = z // 4
        h = z % 4
        to_z = 4 * c + i
        step = step_of(g, m)
        return (
            src.at[pl.ds(m * chunk, chunk)], back.at[h, chunk_rows(step)],
            osem.at[g, i, m], bsem.at[h, (y + step) % NY],
            line + to_z, y * 2 + core, jnp.logical_and(to_z == z, core == c),
        )

    def q_trade():
        return push(qb.at[edge], q_in, qxsem, qxrsem, beyond, mate)

    def o_trade(g):
        return push(ob.at[g, edge], edge_in.at[g], oxsem.at[g], oxrsem.at[g], beyond, mate)

    @pl.when(owner)
    def _():
        pump_sides(0)
        pump_line(2)
        pump_sides(1)
        pump_line(3)
        pump_sides(2)
        pump_sides(3)
        push(qb.at[edge], qb.at[edge], fsem.at[0], qsem.at[edge], blk, mate).wait_recv()
        q_trade().start()
        for n in range(1, 4):
            i = (edge + n) % 4
            push(qb.at[i], qb.at[i], fsem.at[0], qsem.at[i], blk, mate).wait_recv()
        for stage_no in range(4):
            pump_across(stage_no)
        rest = kv.at[pl.ds(0, 13)]
        push(rest, rest, fsem.at[0], matesem, blk, mate).wait_recv()
        factor = 1.4426950408889634 / (HD**0.5)
        end = line + 4 * c + edge
        swapped = jnp.clip((map_ref[end] - end) * (2 * c - 1), 0, 1)

        def settle(g):
            o_trade(g).wait_recv()
            edge_out[g] = jnp.where(swapped > 0, edge_in[g], ob[g, edge])
            for m in (0, 1):
                give(*o_out(g, edge, m, edge_out.at[g]))

        def half_tile(turn_no, _):
            g = turn_no // 4
            r = turn_no % 4
            ends = r == 2 - 2 * g
            n = jnp.where(g == 0, jnp.where(r == 3, 2, r), r - 1)
            i = jnp.where(ends, edge, (edge + 1 + (n + z) % 3) % 4)
            other = jnp.where(ends, 1, 0) * swapped
            position = line + 4 * c + i + other * (2 * c - 1)
            row0 = corner_ref[0, position]
            col0 = corner_ref[1, position]
            spans = [chunk_rows(step_of(g, m)) for m in (0, 1)]
            for m in (0, 1):
                q_now[pl.ds(m * chunk, chunk), :] = qb[i, spans[m], :]

            @pl.when(turn_no == 2)
            def _():
                q_trade().wait_recv()

            @pl.when(ends)
            def _():
                for m in (0, 1):
                    q_now[pl.ds(m * chunk, chunk), :] = jnp.where(
                        swapped > 0, q_in[spans[m], :], qb[edge, spans[m], :]
                    )

            queries = q_now[...]
            slots = []
            best = None
            for w in range(WIN * WIN):
                slot = map_ref[(row0 + w // WIN) * GW + col0 + w % WIN]
                slots.append(slot)
                s = lax.dot_general(
                    queries, kv[slot, 0], (((1,), (1,)), ((), ())),
                    preferred_element_type=jnp.float32,
                )
                scores[w] = s
                for m in range(TILE // HD):
                    part = s[:, m * HD : (m + 1) * HD]
                    best = part if best is None else jnp.maximum(best, part)
            highest = jnp.max(best, axis=-1, keepdims=True)
            total = jnp.zeros((2 * chunk, HD), jnp.float32)
            accum = jnp.zeros((2 * chunk, HD), jnp.float32)
            for w in range(WIN * WIN):
                probs = jnp.exp2((scores[w] - highest) * factor)
                for m in range(TILE // HD):
                    total = total + probs[:, m * HD : (m + 1) * HD]
                accum = accum + jnp.dot(
                    probs.astype(jnp.bfloat16), kv[slots[w], 1],
                    preferred_element_type=jnp.float32,
                )
            denom = jnp.sum(total, axis=-1, keepdims=True)
            ob[g, i] = (accum / denom).astype(ob.dtype)

            @pl.when(ends)
            def _():
                o_trade(g).start()

            @pl.when(jnp.logical_not(ends))
            def _():
                for m in (0, 1):
                    give(*o_out(g, i, m, ob.at[g, i]))

            @pl.when(turn_no == 4)
            def _():
                settle(0)

            return 0

        lax.fori_loop(0, 8, half_tile, 0)
        settle(1)

    weights[-1].wait()
    mates = []

    def out_block(n):
        step = order[n]
        for h in range(heads):
            ref = back.at[h, chunk_rows(step)]
            push(ref, ref, fsem.at[0], bsem.at[h, (y + step) % NY], blk, mate).wait_recv()
        for k, core in enumerate((1 - c, c)):
            u = ((y + step) % NY) * 2 + core
            for h in range(heads):
                lhs[n, pl.ds(k * rows, rows), pl.ds(h * HD, HD)] = back[
                    h, pl.ds(pl.multiple_of(u * rows, 16), rows), :
                ]
        part = jnp.dot(lhs[n], wo[...], preferred_element_type=jnp.float32)
        give_mate[n] = part[:rows].astype(give_mate.dtype)
        copy = push(give_mate.at[n], from_mate.at[n], msem.at[n], mrsem.at[n], blk, mate)
        copy.start()
        mates.append(copy)
        acc[n] = part[rows:]

    def cols(k):
        return slice(k * half, (k + 1) * half)

    def mixed(n, k):
        return acc[n, :, cols(k)] + from_mate[n, :, cols(k)].astype(jnp.float32)

    sent = []

    def relay(k, to):
        relay_out[k] = mixed(0, k).astype(relay_out.dtype)
        copy = push(relay_out.at[k], relay_in.at[k], ssem.at[k], rsem.at[k], blk, to)
        copy.start()
        sent.append(copy)

    def finish(d, k, to, extra):
        value = mixed(1 + d, k)
        if extra is not None:
            value = value + extra
        fin_out[d, k] = value.astype(fin_out.dtype)
        n = 2 + d * 2 + k
        copy = push(fin_out.at[d, k], fin_in.at[d, k], ssem.at[n], rsem.at[n], blk, to)
        copy.start()
        sent.append(copy)

    out_block(0)
    mates[0].wait_recv()
    relay(0, up)
    relay(1, dn)
    out_block(1)
    mates[1].wait_recv()
    finish(0, 1, up, None)
    out_block(2)
    mates[2].wait_recv()
    finish(1, 0, dn, None)
    for d, to in ((0, up), (1, dn)):
        sent[d].wait_recv()
        finish(d, d, to, relay_in[d].astype(jnp.float32))
    out_block(3)
    mates[3].wait_recv()
    for copy in sent[2:]:
        copy.wait_recv()
    for k in (0, 1):
        total = mixed(3, k) + fin_in[0, k].astype(jnp.float32) + fin_in[1, k].astype(jnp.float32)
        out_ref[:, cols(k)] = (gate_ref[:, cols(k)] * total).astype(out_ref.dtype)

    for copy in gathered + sent + mates:
        copy.wait_send()
    for n in range(heads):
        for stage_no in range(4):
            for b in range(len(blocks(stage_no))):
                given(*kv_out(n, stage_no, b))
                given(*q_out(n, stage_no, b))

    @pl.when(owner)
    def _():
        q_trade().wait_send()
        for kind in range(7):
            tiles = 1 if kind in (FAR, MATE_ACROSS) else 4
            ref = kv.at[pl.ds(0, tiles)]
            push(ref, ref, fsem.at[kind], matesem, blk, mate).wait_send()
        for g in (0, 1):
            o_trade(g).wait_send()
            for i in range(4):
                for m in (0, 1):
                    given(*o_out(g, i, m, edge_out.at[g]))


def vmem():
    return pl.BlockSpec(memory_space=pltpu.VMEM)


def hbm():
    return pl.BlockSpec(memory_space=pl.ANY)


def smem():
    return pl.BlockSpec(memory_space=pltpu.SMEM)


def on_device(tokens, mod_shift, mod_scale, out_gate, w_qkv, w_out, tile_map, window_corner):
    rows, width = tokens.shape
    heads = w_qkv.shape[1]
    bf16 = jnp.bfloat16
    f32 = jnp.float32
    dma = pltpu.SemaphoreType.DMA
    return pl.pallas_call(
        block_kernel,
        out_shape=jax.ShapeDtypeStruct((rows, width), bf16),
        in_specs=[smem(), smem(), vmem(), vmem(), vmem(), vmem(), hbm(), hbm()],
        out_specs=vmem(),
        scratch_shapes=[
            pltpu.VMEM((TILE, width), bf16),
            pltpu.VMEM((heads, width, 2 * HD), bf16),
            pltpu.VMEM((width, heads * HD), bf16),
            pltpu.VMEM((heads * HD, width), bf16),
            pltpu.VMEM((heads, 3, TILE, HD), bf16),
            pltpu.VMEM((NX * NZ, 2, TILE, HD), bf16),
            pltpu.VMEM((4, TILE, HD), bf16),
            pltpu.VMEM((TILE, HD), bf16),
            pltpu.VMEM((TILE // 2, HD), bf16),
            pltpu.VMEM((2, 4, TILE // 2, HD), bf16),
            pltpu.VMEM((2, TILE // 2, HD), bf16),
            pltpu.VMEM((2, TILE // 2, HD), bf16),
            pltpu.VMEM((heads, TILE, HD), bf16),
            pltpu.VMEM((WIN * WIN, TILE // 2, TILE), f32),
            pltpu.VMEM((4, 2 * rows, heads * HD), bf16),
            pltpu.VMEM((4, rows, width), f32),
            pltpu.VMEM((4, rows, width), bf16),
            pltpu.VMEM((4, rows, width), bf16),
            pltpu.VMEM((2, rows, width // 2), bf16),
            pltpu.VMEM((2, rows, width // 2), bf16),
            pltpu.VMEM((2, 2, rows, width // 2), bf16),
            pltpu.VMEM((2, 2, rows, width // 2), bf16),
            dma((6,)),
            dma,
            dma((14,)),
            dma((8, 2)),
            dma((3, 4, 2)),
            dma((3, 4, 2)),
            dma((NX * NZ, 4)),
            dma,
            dma((7,)),
            dma((4,)),
            dma((3, 4)),
            dma((2, 4, 2)),
            dma,
            dma,
            dma((2,)),
            dma((2,)),
            dma((4,)),
            dma((4,)),
            dma((6,)),
            dma((6,)),
        ],
        compiler_params=pltpu.CompilerParams(
            collective_id=0, has_side_effects=True, vmem_limit_bytes=VMEM_LIMIT
        ),
        name="block",
    )(
        tile_map, window_corner.T, tokens, mod_shift[None, :], mod_scale[None, :],
        out_gate[None, :], jnp.transpose(w_qkv, (1, 0, 2)), w_out,
    )


def solution(mesh):
    in_specs = (
        P(("blk", "uly"), None),
        P(),
        P(),
        P(),
        P(None, "uly", None),
        P("uly", None),
        P(),
        P(),
    )
    out_specs = P(("blk", "uly"), None)
    return jax.shard_map(
        on_device, mesh=mesh, in_specs=in_specs, out_specs=out_specs, check_vma=False
    )
```

```python
import jax
import jax.numpy as jnp
from jax import lax
from jax.experimental import pallas as pl
from jax.experimental.pallas import tpu as pltpu
from jax.sharding import PartitionSpec as P

TILE = 384
WIN = 3
GW = 4
NX = 4
NZ = 8
NY = 4
HD = 128
MESH = pl.DeviceIdType.MESH
VMEM_LIMIT = 62 * 1024 * 1024


def push(src, dst, send_sem, recv_sem, blk, uly):
    return pltpu.make_async_remote_copy(
        src_ref=src,
        dst_ref=dst,
        send_sem=send_sem,
        recv_sem=recv_sem,
        device_id={"blk": blk, "uly": uly},
        device_id_type=MESH,
    )


def block_kernel(
    map_ref, corner_ref, x_ref, shift_ref, scale_ref, gate_ref, w_hbm, wo_hbm, out_ref,
    xbuf, wkv, wq, wo, stage, kv, qb, q_in, q_now, ob, edge_in, edge_out, back, scores,
    lhs, acc, give_mate, from_mate, relay_out, relay_in, fin_out, fin_in,
    wsem, wosem, gsem, grsem, asem, aqsem, kvsem, matesem, fsem, qsem, bsem, osem,
    qxsem, qxrsem, oxsem, oxrsem, msem, mrsem, ssem, rsem, mixed_out, outsem,
):
    blk = lax.axis_index("blk")
    uly = lax.axis_index("uly")
    y, c = uly // 2, uly % 2
    x, z = blk // NZ, blk % NZ
    line = x * NZ
    rows, width = x_ref.shape
    half = width // 2
    chunk = 2 * rows
    heads = w_hbm.shape[0]
    up = ((y + 1) % NY) * 2 + c
    dn = ((y + 3) % NY) * 2 + c
    ahead = (y + 1 + 2 * c) % NY
    behind = (y + 3 + 2 * c) % NY
    onward = ahead * 2 + c
    mate = y * 2 + (1 - c)
    x_up = ((x + 1) % NX) * NZ + z
    x_dn = ((x + 3) % NX) * NZ + z
    x_far = ((x + 2) % NX) * NZ + z
    owner = z % 4 != 3
    beyond = ((x + 3 + 2 * c) % NX) * NZ + z
    edge = 3 * c

    weights = []
    for h in range(heads):
        weights.append(
            pltpu.make_async_copy(w_hbm.at[h, :, pl.ds(HD, 2 * HD)], wkv.at[h], wsem.at[h])
        )
    for h in range(heads):
        weights.append(
            pltpu.make_async_copy(
                w_hbm.at[h, :, pl.ds(0, HD)], wq.at[:, pl.ds(h * HD, HD)], wsem.at[heads + h]
            )
        )
    weights.append(pltpu.make_async_copy(wo_hbm, wo, wosem))
    for copy in weights:
        copy.start()

    peers = [(blk, mate), (blk, up), (blk, dn), (x_up, uly), (x_dn, uly), (x_far, uly), (beyond, mate)]
    for step in range(1, NZ):
        for core in (0, 1):
            peers.append((line + (z + step) % NZ, y * 2 + core))
    barrier = pltpu.get_barrier_semaphore()
    for to_blk, to_uly in peers:
        pl.semaphore_signal(
            barrier, inc=1, device_id={"blk": to_blk, "uly": to_uly}, device_id_type=MESH
        )

    values = x_ref[...].astype(jnp.float32)
    mean = jnp.mean(values, axis=-1, keepdims=True)
    centred = values - mean
    var = jnp.mean(centred * centred, axis=-1, keepdims=True)
    normed = centred * lax.rsqrt(var + 1e-06) * (1.0 + scale_ref[...]) + shift_ref[...]
    xbuf[pl.ds(pl.multiple_of(uly * rows, 16), rows), :] = normed.astype(xbuf.dtype)

    pl.semaphore_wait(barrier, len(peers))

    def piece(u, k):
        return xbuf.at[
            pl.ds(pl.multiple_of(u * rows, 16), rows), pl.ds(pl.multiple_of(k * half, 128), half)
        ]

    gathered = []

    def spread(u, k, to):
        copy = push(piece(u, k), piece(u, k), gsem.at[len(gathered)], grsem.at[u, k], blk, to)
        copy.start()
        gathered.append(copy)

    def arrive(u, k):
        push(piece(u, k), piece(u, k), gsem.at[0], grsem.at[u, k], blk, mate).wait_recv()

    def chunk_rows(step):
        return pl.ds(pl.multiple_of(((y + step) % NY) * chunk, 16), chunk)

    def blocks(stage_no):
        if stage_no in (0, 3):
            return [chunk_rows(2 if stage_no else 0)]
        return [
            pl.ds(pl.multiple_of(u * rows, 16), rows)
            for u in (((y + 3) % NY) * 2 + stage_no - 1, ((y + 1) % NY) * 2 + 2 - stage_no)
        ]

    def give(src, dst, send_sem, recv_sem, to_blk, to_uly, is_self):
        @pl.when(jnp.logical_not(is_self))
        def _():
            push(src, dst, send_sem, recv_sem, to_blk, to_uly).start()

        @pl.when(is_self)
        def _():
            pltpu.make_async_copy(src, dst, recv_sem).start()

    def given(src, dst, send_sem, recv_sem, to_blk, to_uly, is_self):
        @pl.when(jnp.logical_not(is_self))
        def _():
            push(src, dst, send_sem, recv_sem, to_blk, to_uly).wait_send()

    def turn(n):
        return (z + n) % heads

    def kv_out(n, stage_no, b):
        h = turn(n)
        zd = 4 * c + h
        core = z % 2
        at = blocks(stage_no)[b]
        return (
            stage.at[h, pl.ds(1, 2), at], kv.at[blk, :, at], asem.at[n, stage_no, b],
            kvsem.at[blk, stage_no],
            line + zd, y * 2 + core, jnp.logical_and(zd == z, core == c),
        )

    def q_out(n, stage_no, b):
        h = turn(n)
        zd = 4 * c + h
        core = z // 4
        at = blocks(stage_no)[b]
        return (
            stage.at[h, 0, at], qb.at[z % 4, at], aqsem.at[n, stage_no, b], qsem.at[z % 4],
            line + zd, y * 2 + core, jnp.logical_and(zd == z, core == c),
        )

    def gather_rows(spans):
        return jnp.concatenate([xbuf[span, :] for span in spans], axis=0)

    def project(stage_no):
        spans = blocks(stage_no)
        left = gather_rows(spans)
        for h in range(heads):
            result = jnp.dot(left, wkv[h], preferred_element_type=jnp.float32)
            for b, span in enumerate(spans):
                for part in (0, 1):
                    stage[h, 1 + part, span, :] = result[
                        b * span.size : (b + 1) * span.size, part * HD : (part + 1) * HD
                    ].astype(stage.dtype)
        for n in range(heads):
            for b in range(len(spans)):
                give(*kv_out(n, stage_no, b))

    def project_queries(stages):
        spans = [span for stage_no in stages for span in blocks(stage_no)]
        result = jnp.dot(gather_rows(spans), wq[...], preferred_element_type=jnp.float32)
        done = 0
        for span in spans:
            for h in range(heads):
                stage[h, 0, span, :] = result[
                    done : done + span.size, h * HD : (h + 1) * HD
                ].astype(stage.dtype)
            done += span.size
        for n in range(heads):
            for stage_no in stages:
                for b in range(len(blocks(stage_no))):
                    give(*q_out(n, stage_no, b))

    odd = (z + c) % 2
    mine = []
    for even_gap, odd_gap in ((0, 1), (2, 7), (6, 3), (4, 5)):
        mine.append((z + even_gap + odd * (odd_gap - even_gap)) % NZ)
    X_UP, X_DN, MATE_LINE, MATE_BELOW, MATE_ABOVE, FAR, MATE_ACROSS = range(7)

    def kv_wait(slot, stage_no):
        ref = kv.at[slot, :, chunk_rows(0)]
        push(ref, ref, fsem.at[0], kvsem.at[slot, stage_no], blk, mate).wait_recv()

    def kv_pass(slot, stage_no, kind, to_blk, to_uly, recv_sem):
        for at in blocks(stage_no):
            ref = kv.at[slot, :, at]
            push(ref, ref, fsem.at[kind], recv_sem, to_blk, to_uly).start()

    def pump_line(stage_no):
        for zs in mine:
            slot = line + zs
            kv_wait(slot, stage_no)
            kv_pass(slot, stage_no, X_UP, x_up, uly, kvsem.at[slot, stage_no])
            kv_pass(slot, stage_no, X_DN, x_dn, uly, kvsem.at[slot, stage_no])
            kv_pass(slot, stage_no, MATE_LINE, blk, mate, matesem)
        if stage_no == 3:
            last = line + 7 * c
            kv_pass(last, stage_no, FAR, x_far, uly, kvsem.at[last, stage_no])

    def pump_sides(stage_no):
        for zs in mine:
            below = ((x + 3) % NX) * NZ + zs
            above = ((x + 1) % NX) * NZ + zs
            kv_wait(below, stage_no)
            kv_pass(below, stage_no, MATE_BELOW, blk, mate, matesem)
            kv_wait(above, stage_no)
            kv_pass(above, stage_no, MATE_ABOVE, blk, mate, matesem)
        if stage_no < 3:
            last = ((x + 1 + 2 * c) % NX) * NZ + 7 * c
            kv_pass(last, stage_no, FAR, beyond, uly, kvsem.at[last, stage_no])

    def pump_across(stage_no):
        across = ((x + 2) % NX) * NZ + 7 * c
        kv_wait(across, stage_no)
        kv_pass(across, stage_no, MATE_ACROSS, blk, mate, matesem)

    for k in (c, 1 - c):
        spread(uly, k, onward)
        spread(uly, k, mate)
    for k in (c, 1 - c):
        arrive(mate, k)
        spread(mate, k, onward)
    for h in range(heads):
        weights[h].wait()
    project(0)
    for h in range(heads):
        weights[heads + h].wait()
    project_queries((0,))
    for stage_no, core in ((1, c), (2, 1 - c)):
        arrive(behind * 2 + core, c)
        spread(behind * 2 + core, c, onward)
        spread(behind * 2 + core, c, mate)
        arrive(behind * 2 + core, 1 - c)
        spread(behind * 2 + core, 1 - c, mate)
        for k in (1 - c, c):
            arrive(ahead * 2 + 1 - core, k)
        project(stage_no)

    @pl.when(owner)
    def _():
        pump_line(0)

    across = ((y + 2) % NY) * 2
    for core in (c, 1 - c):
        arrive(across + core, c)
        spread(across + core, c, mate)
    for core in (1 - c, c):
        arrive(across + core, 1 - c)
    project(3)

    @pl.when(owner)
    def _():
        pump_line(1)

    project_queries((1, 2, 3))

    order = (2, 1, 3, 0)

    def step_of(g, m):
        return 2 + g if m == 0 else 1 - g + NY

    def o_out(g, i, m, src):
        core = z // 4
        h = z % 4
        to_z = 4 * c + i
        step = step_of(g, m)
        return (
            src.at[pl.ds(m * chunk, chunk)], back.at[h, chunk_rows(step)],
            osem.at[g, i, m], bsem.at[h, (y + step) % NY],
            line + to_z, y * 2 + core, jnp.logical_and(to_z == z, core == c),
        )

    def q_trade():
        return push(qb.at[edge], q_in, qxsem, qxrsem, beyond, mate)

    def o_trade(g):
        return push(ob.at[g, edge], edge_in.at[g], oxsem.at[g], oxrsem.at[g], beyond, mate)

    @pl.when(owner)
    def _():
        pump_sides(0)
        pump_line(2)
        pump_sides(1)
        pump_line(3)
        pump_sides(2)
        pump_sides(3)
        push(qb.at[edge], qb.at[edge], fsem.at[0], qsem.at[edge], blk, mate).wait_recv()
        q_trade().start()
        for n in range(1, 4):
            i = (edge + n) % 4
            push(qb.at[i], qb.at[i], fsem.at[0], qsem.at[i], blk, mate).wait_recv()
        for stage_no in range(4):
            pump_across(stage_no)
        rest = kv.at[pl.ds(0, 13)]
        push(rest, rest, fsem.at[0], matesem, blk, mate).wait_recv()
        factor = 1.4426950408889634 / (HD**0.5)
        end = line + 4 * c + edge
        swapped = jnp.clip((map_ref[end] - end) * (2 * c - 1), 0, 1)

        def settle(g):
            o_trade(g).wait_recv()
            edge_out[g] = jnp.where(swapped > 0, edge_in[g], ob[g, edge])
            for m in (0, 1):
                give(*o_out(g, edge, m, edge_out.at[g]))

        def half_tile(turn_no, _):
            g = turn_no // 4
            r = turn_no % 4
            ends = r == 2 - 2 * g
            n = jnp.where(g == 0, jnp.where(r == 3, 2, r), r - 1)
            i = jnp.where(ends, edge, (edge + 1 + (n + z) % 3) % 4)
            other = jnp.where(ends, 1, 0) * swapped
            position = line + 4 * c + i + other * (2 * c - 1)
            row0 = corner_ref[0, position]
            col0 = corner_ref[1, position]
            spans = [chunk_rows(step_of(g, m)) for m in (0, 1)]
            for m in (0, 1):
                q_now[pl.ds(m * chunk, chunk), :] = qb[i, spans[m], :]

            @pl.when(turn_no == 2)
            def _():
                q_trade().wait_recv()

            @pl.when(ends)
            def _():
                for m in (0, 1):
                    q_now[pl.ds(m * chunk, chunk), :] = jnp.where(
                        swapped > 0, q_in[spans[m], :], qb[edge, spans[m], :]
                    )

            queries = q_now[...]
            slots = []
            best = None
            for w in range(WIN * WIN):
                slot = map_ref[(row0 + w // WIN) * GW + col0 + w % WIN]
                slots.append(slot)
                s = lax.dot_general(
                    queries, kv[slot, 0], (((1,), (1,)), ((), ())),
                    preferred_element_type=jnp.float32,
                )
                scores[w] = s
                for m in range(TILE // HD):
                    part = s[:, m * HD : (m + 1) * HD]
                    best = part if best is None else jnp.maximum(best, part)
            highest = jnp.max(best, axis=-1, keepdims=True)
            total = jnp.zeros((2 * chunk, HD), jnp.float32)
            accum = jnp.zeros((2 * chunk, HD), jnp.float32)
            for w in range(WIN * WIN):
                probs = jnp.exp2((scores[w] - highest) * factor)
                for m in range(TILE // HD):
                    total = total + probs[:, m * HD : (m + 1) * HD]
                accum = accum + jnp.dot(
                    probs.astype(jnp.bfloat16), kv[slots[w], 1],
                    preferred_element_type=jnp.float32,
                )
            denom = jnp.sum(total, axis=-1, keepdims=True)
            ob[g, i] = (accum / denom).astype(ob.dtype)

            @pl.when(ends)
            def _():
                o_trade(g).start()

            @pl.when(jnp.logical_not(ends))
            def _():
                for m in (0, 1):
                    give(*o_out(g, i, m, ob.at[g, i]))

            @pl.when(turn_no == 4)
            def _():
                settle(0)

            return 0

        lax.fori_loop(0, 8, half_tile, 0)
        settle(1)

    weights[-1].wait()
    mates = []

    def out_block(n):
        step = order[n]
        for h in range(heads):
            ref = back.at[h, chunk_rows(step)]
            push(ref, ref, fsem.at[0], bsem.at[h, (y + step) % NY], blk, mate).wait_recv()
        for k, core in enumerate((1 - c, c)):
            u = ((y + step) % NY) * 2 + core
            for h in range(heads):
                lhs[n, pl.ds(k * rows, rows), pl.ds(h * HD, HD)] = back[
                    h, pl.ds(pl.multiple_of(u * rows, 16), rows), :
                ]
        part = jnp.dot(lhs[n], wo[...], preferred_element_type=jnp.float32)
        give_mate[n] = part[:rows].astype(give_mate.dtype)
        copy = push(give_mate.at[n], from_mate.at[n], msem.at[n], mrsem.at[n], blk, mate)
        copy.start()
        mates.append(copy)
        acc[n] = part[rows:]

    def cols(k):
        return slice(k * half, (k + 1) * half)

    def mixed(n, k):
        return acc[n, :, cols(k)] + from_mate[n, :, cols(k)].astype(jnp.float32)

    sent = []

    def relay(k, to):
        relay_out[k] = mixed(0, k).astype(relay_out.dtype)
        copy = push(relay_out.at[k], relay_in.at[k], ssem.at[k], rsem.at[k], blk, to)
        copy.start()
        sent.append(copy)

    def finish(d, k, to, extra):
        value = mixed(1 + d, k)
        if extra is not None:
            value = value + extra
        fin_out[d, k] = value.astype(fin_out.dtype)
        n = 2 + d * 2 + k
        copy = push(fin_out.at[d, k], fin_in.at[d, k], ssem.at[n], rsem.at[n], blk, to)
        copy.start()
        sent.append(copy)

    out_block(0)
    mates[0].wait_recv()
    relay(0, up)
    relay(1, dn)
    out_block(1)
    mates[1].wait_recv()
    finish(0, 1, up, None)
    out_block(2)
    mates[2].wait_recv()
    finish(1, 0, dn, None)
    for d, to in ((0, up), (1, dn)):
        sent[d].wait_recv()
        finish(d, d, to, relay_in[d].astype(jnp.float32))
    out_block(3)
    mates[3].wait_recv()
    for copy in sent[2:]:
        copy.wait_recv()
    for k in (0, 1):
        total = mixed(3, k) + fin_in[0, k].astype(jnp.float32) + fin_in[1, k].astype(jnp.float32)
        mixed_out[:, cols(k)] = (gate_ref[:, cols(k)] * total).astype(mixed_out.dtype)

    result_copy = pltpu.make_async_copy(mixed_out, out_ref, outsem)
    result_copy.start()

    for copy in gathered + sent + mates:
        copy.wait_send()
    for n in range(heads):
        for stage_no in range(4):
            for b in range(len(blocks(stage_no))):
                given(*kv_out(n, stage_no, b))
                given(*q_out(n, stage_no, b))

    @pl.when(owner)
    def _():
        q_trade().wait_send()
        for kind in range(7):
            tiles = 1 if kind in (FAR, MATE_ACROSS) else 4
            ref = kv.at[pl.ds(0, tiles)]
            push(ref, ref, fsem.at[kind], matesem, blk, mate).wait_send()
        for g in (0, 1):
            o_trade(g).wait_send()
            for i in range(4):
                for m in (0, 1):
                    given(*o_out(g, i, m, edge_out.at[g]))

    result_copy.wait()


def vmem():
    return pl.BlockSpec(memory_space=pltpu.VMEM)


def hbm():
    return pl.BlockSpec(memory_space=pl.ANY)


def smem():
    return pl.BlockSpec(memory_space=pltpu.SMEM)


def on_device(tokens, mod_shift, mod_scale, out_gate, w_qkv, w_out, tile_map, window_corner):
    rows, width = tokens.shape
    heads = w_qkv.shape[1]
    bf16 = jnp.bfloat16
    f32 = jnp.float32
    dma = pltpu.SemaphoreType.DMA
    return pl.pallas_call(
        block_kernel,
        out_shape=jax.ShapeDtypeStruct((rows, width), bf16),
        in_specs=[smem(), smem(), vmem(), vmem(), vmem(), vmem(), hbm(), hbm()],
        out_specs=hbm(),
        scratch_shapes=[
            pltpu.VMEM((TILE, width), bf16),
            pltpu.VMEM((heads, width, 2 * HD), bf16),
            pltpu.VMEM((width, heads * HD), bf16),
            pltpu.VMEM((heads * HD, width), bf16),
            pltpu.VMEM((heads, 3, TILE, HD), bf16),
            pltpu.VMEM((NX * NZ, 2, TILE, HD), bf16),
            pltpu.VMEM((4, TILE, HD), bf16),
            pltpu.VMEM((TILE, HD), bf16),
            pltpu.VMEM((TILE // 2, HD), bf16),
            pltpu.VMEM((2, 4, TILE // 2, HD), bf16),
            pltpu.VMEM((2, TILE // 2, HD), bf16),
            pltpu.VMEM((2, TILE // 2, HD), bf16),
            pltpu.VMEM((heads, TILE, HD), bf16),
            pltpu.VMEM((WIN * WIN, TILE // 2, TILE), f32),
            pltpu.VMEM((4, 2 * rows, heads * HD), bf16),
            pltpu.VMEM((4, rows, width), f32),
            pltpu.VMEM((4, rows, width), bf16),
            pltpu.VMEM((4, rows, width), bf16),
            pltpu.VMEM((2, rows, width // 2), bf16),
            pltpu.VMEM((2, rows, width // 2), bf16),
            pltpu.VMEM((2, 2, rows, width // 2), bf16),
            pltpu.VMEM((2, 2, rows, width // 2), bf16),
            dma((6,)),
            dma,
            dma((14,)),
            dma((8, 2)),
            dma((3, 4, 2)),
            dma((3, 4, 2)),
            dma((NX * NZ, 4)),
            dma,
            dma((7,)),
            dma((4,)),
            dma((3, 4)),
            dma((2, 4, 2)),
            dma,
            dma,
            dma((2,)),
            dma((2,)),
            dma((4,)),
            dma((4,)),
            dma((6,)),
            dma((6,)),
            pltpu.VMEM((rows, width), bf16),
            dma,
        ],
        compiler_params=pltpu.CompilerParams(
            collective_id=0, has_side_effects=True, vmem_limit_bytes=VMEM_LIMIT
        ),
        name="block",
    )(
        tile_map, window_corner.T, tokens, mod_shift[None, :], mod_scale[None, :],
        out_gate[None, :], jnp.transpose(w_qkv, (1, 0, 2)), w_out,
    )


def solution(mesh):
    in_specs = (
        P(("blk", "uly"), None),
        P(),
        P(),
        P(),
        P(None, "uly", None),
        P("uly", None),
        P(),
        P(),
    )
    out_specs = P(("blk", "uly"), None)
    return jax.shard_map(
        on_device, mesh=mesh, in_specs=in_specs, out_specs=out_specs, check_vma=False
    )
```

```python
import jax
import jax.numpy as jnp
from jax import lax
from jax.experimental import pallas as pl
from jax.experimental.pallas import tpu as pltpu
from jax.sharding import PartitionSpec as P

TILE = 384
WIN = 3
GW = 4
NX = 4
NZ = 8
NY = 4
HD = 128
MESH = pl.DeviceIdType.MESH
VMEM_LIMIT = 62 * 1024 * 1024


def push(src, dst, send_sem, recv_sem, blk, uly):
    return pltpu.make_async_remote_copy(
        src_ref=src,
        dst_ref=dst,
        send_sem=send_sem,
        recv_sem=recv_sem,
        device_id={"blk": blk, "uly": uly},
        device_id_type=MESH,
    )


def block_kernel(
    map_ref, corner_ref, x_ref, shift_ref, scale_ref, gate_ref, w_hbm, wo_hbm, out_ref,
    xbuf, wkv, wq, wo, stage, kv, qb, q_in, q_now, ob, edge_in, edge_out, back, scores,
    lhs, acc, give_mate, from_mate, relay_out, relay_in, fin_out, fin_in,
    wsem, wosem, gsem, grsem, asem, aqsem, kvsem, matesem, fsem, qsem, bsem, osem,
    qxsem, qxrsem, oxsem, oxrsem, msem, mrsem, ssem, rsem, mixed_out, outsem,
):
    blk = lax.axis_index("blk")
    uly = lax.axis_index("uly")
    y, c = uly // 2, uly % 2
    x, z = blk // NZ, blk % NZ
    line = x * NZ
    rows, width = x_ref.shape
    half = width // 2
    chunk = 2 * rows
    heads = w_hbm.shape[0]
    up = ((y + 1) % NY) * 2 + c
    dn = ((y + 3) % NY) * 2 + c
    ahead = (y + 1 + 2 * c) % NY
    behind = (y + 3 + 2 * c) % NY
    onward = ahead * 2 + c
    mate = y * 2 + (1 - c)
    x_up = ((x + 1) % NX) * NZ + z
    x_dn = ((x + 3) % NX) * NZ + z
    x_far = ((x + 2) % NX) * NZ + z
    owner = z % 4 != 3
    beyond = ((x + 3 + 2 * c) % NX) * NZ + z
    edge = 3 * c

    weights = []
    for h in range(heads):
        weights.append(
            pltpu.make_async_copy(w_hbm.at[h, :, pl.ds(HD, 2 * HD)], wkv.at[h], wsem.at[h])
        )
    for h in range(heads):
        weights.append(
            pltpu.make_async_copy(
                w_hbm.at[h, :, pl.ds(0, HD)], wq.at[:, pl.ds(h * HD, HD)], wsem.at[heads + h]
            )
        )
    weights.append(pltpu.make_async_copy(wo_hbm, wo, wosem))
    for copy in weights:
        copy.start()

    peers = [(blk, mate), (blk, up), (blk, dn), (x_up, uly), (x_dn, uly), (x_far, uly), (beyond, mate)]
    for step in range(1, NZ):
        for core in (0, 1):
            peers.append((line + (z + step) % NZ, y * 2 + core))
    barrier = pltpu.get_barrier_semaphore()
    for to_blk, to_uly in peers:
        pl.semaphore_signal(
            barrier, inc=1, device_id={"blk": to_blk, "uly": to_uly}, device_id_type=MESH
        )

    values = x_ref[...].astype(jnp.float32)
    mean = jnp.mean(values, axis=-1, keepdims=True)
    centred = values - mean
    var = jnp.mean(centred * centred, axis=-1, keepdims=True)
    normed = centred * lax.rsqrt(var + 1e-06) * (1.0 + scale_ref[...]) + shift_ref[...]
    xbuf[pl.ds(pl.multiple_of(uly * rows, 16), rows), :] = normed.astype(xbuf.dtype)

    pl.semaphore_wait(barrier, len(peers))

    def piece(u, k):
        return xbuf.at[
            pl.ds(pl.multiple_of(u * rows, 16), rows), pl.ds(pl.multiple_of(k * half, 128), half)
        ]

    gathered = []

    def spread(u, k, to):
        copy = push(piece(u, k), piece(u, k), gsem.at[len(gathered)], grsem.at[u, k], blk, to)
        copy.start()
        gathered.append(copy)

    def arrive(u, k):
        push(piece(u, k), piece(u, k), gsem.at[0], grsem.at[u, k], blk, mate).wait_recv()

    def chunk_rows(step):
        return pl.ds(pl.multiple_of(((y + step) % NY) * chunk, 16), chunk)

    def blocks(stage_no):
        if stage_no in (0, 3):
            return [chunk_rows(2 if stage_no else 0)]
        return [
            pl.ds(pl.multiple_of(u * rows, 16), rows)
            for u in (((y + 3) % NY) * 2 + stage_no - 1, ((y + 1) % NY) * 2 + 2 - stage_no)
        ]

    def give(src, dst, send_sem, recv_sem, to_blk, to_uly, is_self):
        @pl.when(jnp.logical_not(is_self))
        def _():
            push(src, dst, send_sem, recv_sem, to_blk, to_uly).start()

        @pl.when(is_self)
        def _():
            pltpu.make_async_copy(src, dst, recv_sem).start()

    def given(src, dst, send_sem, recv_sem, to_blk, to_uly, is_self):
        @pl.when(jnp.logical_not(is_self))
        def _():
            push(src, dst, send_sem, recv_sem, to_blk, to_uly).wait_send()

    def turn(n):
        return (z + n) % heads

    def kv_out(n, stage_no, b):
        h = turn(n)
        zd = 4 * c + h
        core = z % 2
        at = blocks(stage_no)[b]
        return (
            stage.at[h, pl.ds(1, 2), at], kv.at[blk, :, at], asem.at[n, stage_no, b],
            kvsem.at[blk, stage_no],
            line + zd, y * 2 + core, jnp.logical_and(zd == z, core == c),
        )

    def q_out(n, stage_no, b):
        h = turn(n)
        zd = 4 * c + h
        core = z // 4
        at = blocks(stage_no)[b]
        return (
            stage.at[h, 0, at], qb.at[z % 4, at], aqsem.at[n, stage_no, b], qsem.at[z % 4],
            line + zd, y * 2 + core, jnp.logical_and(zd == z, core == c),
        )

    def gather_rows(spans):
        return jnp.concatenate([xbuf[span, :] for span in spans], axis=0)

    def project(stage_no):
        spans = blocks(stage_no)
        left = gather_rows(spans)
        for h in range(heads):
            result = jnp.dot(left, wkv[h], preferred_element_type=jnp.float32)
            for b, span in enumerate(spans):
                for part in (0, 1):
                    stage[h, 1 + part, span, :] = result[
                        b * span.size : (b + 1) * span.size, part * HD : (part + 1) * HD
                    ].astype(stage.dtype)
        for n in range(heads):
            for b in range(len(spans)):
                give(*kv_out(n, stage_no, b))

    def project_queries(stages):
        spans = [span for stage_no in stages for span in blocks(stage_no)]
        result = jnp.dot(gather_rows(spans), wq[...], preferred_element_type=jnp.float32)
        done = 0
        for span in spans:
            for h in range(heads):
                stage[h, 0, span, :] = result[
                    done : done + span.size, h * HD : (h + 1) * HD
                ].astype(stage.dtype)
            done += span.size
        for n in range(heads):
            for stage_no in stages:
                for b in range(len(blocks(stage_no))):
                    give(*q_out(n, stage_no, b))

    odd = (z + c) % 2
    mine = []
    for even_gap, odd_gap in ((0, 1), (2, 7), (6, 3), (4, 5)):
        mine.append((z + even_gap + odd * (odd_gap - even_gap)) % NZ)
    X_UP, X_DN, MATE_LINE, MATE_BELOW, MATE_ABOVE, FAR, MATE_ACROSS = range(7)

    def kv_wait(slot, stage_no):
        ref = kv.at[slot, :, chunk_rows(0)]
        push(ref, ref, fsem.at[0], kvsem.at[slot, stage_no], blk, mate).wait_recv()

    def kv_pass(slot, stage_no, kind, to_blk, to_uly, recv_sem):
        for at in blocks(stage_no):
            ref = kv.at[slot, :, at]
            push(ref, ref, fsem.at[kind], recv_sem, to_blk, to_uly).start()

    def pump_line(stage_no):
        for zs in mine:
            slot = line + zs
            kv_wait(slot, stage_no)
            kv_pass(slot, stage_no, X_UP, x_up, uly, kvsem.at[slot, stage_no])
            kv_pass(slot, stage_no, X_DN, x_dn, uly, kvsem.at[slot, stage_no])
            kv_pass(slot, stage_no, MATE_LINE, blk, mate, matesem)
        if stage_no == 3:
            last = line + 7 * c
            kv_pass(last, stage_no, FAR, x_far, uly, kvsem.at[last, stage_no])

    def pump_sides(stage_no):
        for zs in mine:
            below = ((x + 3) % NX) * NZ + zs
            above = ((x + 1) % NX) * NZ + zs
            kv_wait(below, stage_no)
            kv_pass(below, stage_no, MATE_BELOW, blk, mate, matesem)
            kv_wait(above, stage_no)
            kv_pass(above, stage_no, MATE_ABOVE, blk, mate, matesem)
        if stage_no < 3:
            last = ((x + 1 + 2 * c) % NX) * NZ + 7 * c
            kv_pass(last, stage_no, FAR, beyond, uly, kvsem.at[last, stage_no])

    def pump_across(stage_no):
        across = ((x + 2) % NX) * NZ + 7 * c
        kv_wait(across, stage_no)
        kv_pass(across, stage_no, MATE_ACROSS, blk, mate, matesem)

    for k in (c, 1 - c):
        spread(uly, k, onward)
        spread(uly, k, mate)
    for k in (c, 1 - c):
        arrive(mate, k)
        spread(mate, k, onward)
    for h in range(heads):
        weights[h].wait()
    project(0)
    for h in range(heads):
        weights[heads + h].wait()
    project_queries((0,))
    for stage_no, core in ((1, c), (2, 1 - c)):
        arrive(behind * 2 + core, c)
        spread(behind * 2 + core, c, onward)
        spread(behind * 2 + core, c, mate)
        arrive(behind * 2 + core, 1 - c)
        spread(behind * 2 + core, 1 - c, mate)
        for k in (1 - c, c):
            arrive(ahead * 2 + 1 - core, k)
        project(stage_no)

    @pl.when(owner)
    def _():
        pump_line(0)

    across = ((y + 2) % NY) * 2
    for core in (c, 1 - c):
        arrive(across + core, c)
        spread(across + core, c, mate)
    for core in (1 - c, c):
        arrive(across + core, 1 - c)
    project(3)

    @pl.when(owner)
    def _():
        pump_line(1)

    project_queries((1, 2, 3))

    order = (2, 1, 3, 0)

    def step_of(g, m):
        return 2 + g if m == 0 else 1 - g + NY

    def o_out(g, i, m, src):
        core = z // 4
        h = z % 4
        to_z = 4 * c + i
        step = step_of(g, m)
        return (
            src.at[pl.ds(m * chunk, chunk)], back.at[h, chunk_rows(step)],
            osem.at[g, i, m], bsem.at[h, (y + step) % NY],
            line + to_z, y * 2 + core, jnp.logical_and(to_z == z, core == c),
        )

    def q_trade():
        return push(qb.at[edge], q_in, qxsem, qxrsem, beyond, mate)

    def o_trade(g):
        return push(ob.at[g, edge], edge_in.at[g], oxsem.at[g], oxrsem.at[g], beyond, mate)

    @pl.when(owner)
    def _():
        pump_sides(0)
        pump_line(2)
        pump_sides(1)
        pump_line(3)
        pump_sides(2)
        pump_sides(3)
        push(qb.at[edge], qb.at[edge], fsem.at[0], qsem.at[edge], blk, mate).wait_recv()
        q_trade().start()
        for n in range(1, 4):
            i = (edge + n) % 4
            push(qb.at[i], qb.at[i], fsem.at[0], qsem.at[i], blk, mate).wait_recv()
        for stage_no in range(4):
            pump_across(stage_no)
        rest = kv.at[pl.ds(0, 13)]
        push(rest, rest, fsem.at[0], matesem, blk, mate).wait_recv()
        factor = 1.4426950408889634 / (HD**0.5)
        end = line + 4 * c + edge
        swapped = jnp.clip((map_ref[end] - end) * (2 * c - 1), 0, 1)

        def settle(g):
            o_trade(g).wait_recv()
            edge_out[g] = jnp.where(swapped > 0, edge_in[g], ob[g, edge])
            for m in (0, 1):
                give(*o_out(g, edge, m, edge_out.at[g]))

        def half_tile(turn_no, _):
            g = turn_no // 4
            r = turn_no % 4
            ends = r == 2 - 2 * g
            n = jnp.where(g == 0, jnp.where(r == 3, 2, r), r - 1)
            i = jnp.where(ends, edge, (edge + 1 + (n + z) % 3) % 4)
            other = jnp.where(ends, 1, 0) * swapped
            position = line + 4 * c + i + other * (2 * c - 1)
            row0 = corner_ref[0, position]
            col0 = corner_ref[1, position]
            spans = [chunk_rows(step_of(g, m)) for m in (0, 1)]
            for m in (0, 1):
                q_now[pl.ds(m * chunk, chunk), :] = qb[i, spans[m], :]

            @pl.when(turn_no == 2)
            def _():
                q_trade().wait_recv()

            @pl.when(ends)
            def _():
                for m in (0, 1):
                    q_now[pl.ds(m * chunk, chunk), :] = jnp.where(
                        swapped > 0, q_in[spans[m], :], qb[edge, spans[m], :]
                    )

            queries = q_now[...]
            slots = []
            best = None
            for w in range(WIN * WIN):
                slot = map_ref[(row0 + w // WIN) * GW + col0 + w % WIN]
                slots.append(slot)
                s = lax.dot_general(
                    queries, kv[slot, 0], (((1,), (1,)), ((), ())),
                    preferred_element_type=jnp.float32,
                )
                scores[w] = s
                for m in range(TILE // HD):
                    part = s[:, m * HD : (m + 1) * HD]
                    best = part if best is None else jnp.maximum(best, part)
            highest = jnp.max(best, axis=-1, keepdims=True)
            total = jnp.zeros((2 * chunk, HD), jnp.float32)
            accum = jnp.zeros((2 * chunk, HD), jnp.float32)
            for w in range(WIN * WIN):
                probs = jnp.exp2((scores[w] - highest) * factor)
                for m in range(TILE // HD):
                    total = total + probs[:, m * HD : (m + 1) * HD]
                accum = accum + jnp.dot(
                    probs.astype(jnp.bfloat16), kv[slots[w], 1],
                    preferred_element_type=jnp.float32,
                )
            denom = jnp.sum(total, axis=-1, keepdims=True)
            ob[g, i] = (accum / denom).astype(ob.dtype)

            @pl.when(ends)
            def _():
                o_trade(g).start()

            @pl.when(jnp.logical_not(ends))
            def _():
                for m in (0, 1):
                    give(*o_out(g, i, m, ob.at[g, i]))

            @pl.when(turn_no == 4)
            def _():
                settle(0)

            return 0

        lax.fori_loop(0, 8, half_tile, 0)
        settle(1)

    weights[-1].wait()
    mates = []

    def out_block(n):
        step = order[n]
        for h in range(heads):
            ref = back.at[h, chunk_rows(step)]
            push(ref, ref, fsem.at[0], bsem.at[h, (y + step) % NY], blk, mate).wait_recv()
        for k, core in enumerate((1 - c, c)):
            u = ((y + step) % NY) * 2 + core
            for h in range(heads):
                lhs[n, pl.ds(k * rows, rows), pl.ds(h * HD, HD)] = back[
                    h, pl.ds(pl.multiple_of(u * rows, 16), rows), :
                ]
        part = jnp.dot(lhs[n], wo[...], preferred_element_type=jnp.float32)
        give_mate[n] = part[:rows].astype(give_mate.dtype)
        copy = push(give_mate.at[n], from_mate.at[n], msem.at[n], mrsem.at[n], blk, mate)
        copy.start()
        mates.append(copy)
        acc[n] = part[rows:]

    def cols(k):
        return slice(k * half, (k + 1) * half)

    def mixed(n, k):
        return acc[n, :, cols(k)] + from_mate[n, :, cols(k)].astype(jnp.float32)

    sent = []

    def relay(k, to):
        relay_out[k] = mixed(0, k).astype(relay_out.dtype)
        copy = push(relay_out.at[k], relay_in.at[k], ssem.at[k], rsem.at[k], blk, to)
        copy.start()
        sent.append(copy)

    def finish(d, k, to, extra):
        value = mixed(1 + d, k)
        if extra is not None:
            value = value + extra
        fin_out[d, k] = value.astype(fin_out.dtype)
        n = 2 + d * 2 + k
        copy = push(fin_out.at[d, k], fin_in.at[d, k], ssem.at[n], rsem.at[n], blk, to)
        copy.start()
        sent.append(copy)

    out_block(0)
    out_block(1)
    mates[0].wait_recv()
    relay(0, up)
    relay(1, dn)
    mates[1].wait_recv()
    finish(0, 1, up, None)
    out_block(2)
    mates[2].wait_recv()
    finish(1, 0, dn, None)
    for d, to in ((0, up), (1, dn)):
        sent[d].wait_recv()
        finish(d, d, to, relay_in[d].astype(jnp.float32))
    out_block(3)
    mates[3].wait_recv()
    for copy in sent[2:]:
        copy.wait_recv()
    for k in (0, 1):
        total = mixed(3, k) + fin_in[0, k].astype(jnp.float32) + fin_in[1, k].astype(jnp.float32)
        mixed_out[:, cols(k)] = (gate_ref[:, cols(k)] * total).astype(mixed_out.dtype)

    result_copy = pltpu.make_async_copy(mixed_out, out_ref, outsem)
    result_copy.start()

    for copy in gathered + sent + mates:
        copy.wait_send()
    for n in range(heads):
        for stage_no in range(4):
            for b in range(len(blocks(stage_no))):
                given(*kv_out(n, stage_no, b))
                given(*q_out(n, stage_no, b))

    @pl.when(owner)
    def _():
        q_trade().wait_send()
        for kind in range(7):
            tiles = 1 if kind in (FAR, MATE_ACROSS) else 4
            ref = kv.at[pl.ds(0, tiles)]
            push(ref, ref, fsem.at[kind], matesem, blk, mate).wait_send()
        for g in (0, 1):
            o_trade(g).wait_send()
            for i in range(4):
                for m in (0, 1):
                    given(*o_out(g, i, m, edge_out.at[g]))

    result_copy.wait()


def vmem():
    return pl.BlockSpec(memory_space=pltpu.VMEM)


def hbm():
    return pl.BlockSpec(memory_space=pl.ANY)


def smem():
    return pl.BlockSpec(memory_space=pltpu.SMEM)


def on_device(tokens, mod_shift, mod_scale, out_gate, w_qkv, w_out, tile_map, window_corner):
    rows, width = tokens.shape
    heads = w_qkv.shape[1]
    bf16 = jnp.bfloat16
    f32 = jnp.float32
    dma = pltpu.SemaphoreType.DMA
    return pl.pallas_call(
        block_kernel,
        out_shape=jax.ShapeDtypeStruct((rows, width), bf16),
        in_specs=[smem(), smem(), vmem(), vmem(), vmem(), vmem(), hbm(), hbm()],
        out_specs=hbm(),
        scratch_shapes=[
            pltpu.VMEM((TILE, width), bf16),
            pltpu.VMEM((heads, width, 2 * HD), bf16),
            pltpu.VMEM((width, heads * HD), bf16),
            pltpu.VMEM((heads * HD, width), bf16),
            pltpu.VMEM((heads, 3, TILE, HD), bf16),
            pltpu.VMEM((NX * NZ, 2, TILE, HD), bf16),
            pltpu.VMEM((4, TILE, HD), bf16),
            pltpu.VMEM((TILE, HD), bf16),
            pltpu.VMEM((TILE // 2, HD), bf16),
            pltpu.VMEM((2, 4, TILE // 2, HD), bf16),
            pltpu.VMEM((2, TILE // 2, HD), bf16),
            pltpu.VMEM((2, TILE // 2, HD), bf16),
            pltpu.VMEM((heads, TILE, HD), bf16),
            pltpu.VMEM((WIN * WIN, TILE // 2, TILE), f32),
            pltpu.VMEM((4, 2 * rows, heads * HD), bf16),
            pltpu.VMEM((4, rows, width), f32),
            pltpu.VMEM((4, rows, width), bf16),
            pltpu.VMEM((4, rows, width), bf16),
            pltpu.VMEM((2, rows, width // 2), bf16),
            pltpu.VMEM((2, rows, width // 2), bf16),
            pltpu.VMEM((2, 2, rows, width // 2), bf16),
            pltpu.VMEM((2, 2, rows, width // 2), bf16),
            dma((6,)),
            dma,
            dma((14,)),
            dma((8, 2)),
            dma((3, 4, 2)),
            dma((3, 4, 2)),
            dma((NX * NZ, 4)),
            dma,
            dma((7,)),
            dma((4,)),
            dma((3, 4)),
            dma((2, 4, 2)),
            dma,
            dma,
            dma((2,)),
            dma((2,)),
            dma((4,)),
            dma((4,)),
            dma((6,)),
            dma((6,)),
            pltpu.VMEM((rows, width), bf16),
            dma,
        ],
        compiler_params=pltpu.CompilerParams(
            collective_id=0, has_side_effects=True, vmem_limit_bytes=VMEM_LIMIT
        ),
        name="block",
    )(
        tile_map, window_corner.T, tokens, mod_shift[None, :], mod_scale[None, :],
        out_gate[None, :], jnp.transpose(w_qkv, (1, 0, 2)), w_out,
    )


def solution(mesh):
    in_specs = (
        P(("blk", "uly"), None),
        P(),
        P(),
        P(),
        P(None, "uly", None),
        P("uly", None),
        P(),
        P(),
    )
    out_specs = P(("blk", "uly"), None)
    return jax.shard_map(
        on_device, mesh=mesh, in_specs=in_specs, out_specs=out_specs, check_vma=False
    )
```
